32 devices in a mesh: groups: 2 (over y), ctx: 4 (over z), head: 2 (over x), pair: 2 (over core).
Axes of the slice: x: 2, y: 2, z: 4, core: 2. Of those that a mesh axis runs over, the one named last changes fastest.
Arguments:
- student_query: bfloat16 [1024, 4096], P(('groups', 'ctx'), ('head', 'pair')), parts along dimension 0, may hold values from -25 to 25
- teacher_keys: bfloat16 [1024, 1024], P(('groups', 'ctx'), ('head', 'pair')), parts along dimension 0, may hold values from -9 to 9
- teacher_values: bfloat16 [1024, 1024], P(('groups', 'ctx'), ('head', 'pair')), parts along dimension 0, may hold values from -6 to 6
- band_span: int32 [1024], P(('groups', 'ctx')), parts along dimension 0, may hold values from 256 to 1024, as said below
- residual_in: bfloat16 [1024, 4096], P(('groups', 'ctx'), ('head', 'pair')), parts along dimension 0, may hold values from -3 to 3
- norm_gain: float32 [4096], replicated, may hold values from 0.25 to 1.75
- w_gate: bfloat16 [4096, 7168], P('ctx', ('head', 'pair')), may hold values from -0.09375 to 0.09375
- w_up: bfloat16 [4096, 7168], P('ctx', ('head', 'pair')), may hold values from -0.09375 to 0.09375
- w_down: bfloat16 [7168, 4096], P(('head', 'pair'), 'ctx'), may hold values from -0.0625 to 0.0625
- teacher_feats: bfloat16 [1024, 7168], P(('groups', 'ctx'), ('head', 'pair')), parts along dimension 0, may hold values from -31 to 31
- keep_tiles: int32 [1024, 56], P(('groups', 'ctx'), ('head', 'pair')), parts along dimension 0, may hold values from 0 to 1, as said below
Outputs:
- layer_out: bfloat16 [1024, 4096], P(('groups', 'ctx'), ('head', 'pair')), parts along dimension 0
- loss_value: float32 [2], P('groups'), parts along dimension 0
- grad_resid: float32 [1024, 4096], P(('groups', 'ctx'), ('head', 'pair')), parts along dimension 0
The draws below stay inside these ranges and needn't reach their ends.
There are 2 independent parts, one for each index of `groups`. The reference program is written for one: setup_inputs(seed, part) draws one part's arguments, and reference() takes and returns one part's arrays. A program takes and returns all parts, laid end to end along the dimension named above; an argument that names none is the same for every part. Nothing has to cross between parts.
Inputs may be any that keep to these rules, and one draw needn't show every extreme that they name: `band_span`: some token's span equals 1024. `keep_tiles`: the first token keeps every tile.
All inputs are finite; a program needn't handle non-finite values.
Results may differ from the reference program's by a relative error of at most 0.014.
Values may be sent and summed in bfloat16 or wider, within the bound.
No kernel may reach another device: no remote copies, remote signals or barrier semaphores. Data moves between devices by JAX's collectives and lax.ppermute only.
A program may use at most 128 MiB of HBM per device.

```python
import math
import jax
import jax.numpy as jnp
from jax import lax

D = 4096
HEADS = 32
KV_HEADS = 8
HEAD_DIM = 128
FF = 7168
TILE = 128
TOKENS = 512
WINDOW = 1024
GROUP_FF = 1792


def teacher_key_rows(key):
    drawn_keys = jnp.clip(2.0 * jax.random.normal(jax.random.fold_in(key, 101), (TOKENS, KV_HEADS * HEAD_DIM), jnp.float32), -9.0, 9.0)
    return drawn_keys


def draw_teacher_keys(key, part):
    return teacher_key_rows(key).astype(jnp.bfloat16)


def draw_student_query(key, part):
    drawn_query = jnp.clip(jax.random.normal(jax.random.fold_in(key, 7), (TOKENS, D), jnp.float32), -6.0, 6.0)
    return drawn_query.astype(jnp.bfloat16)


def draw_teacher_feats(key, part):
    spread = math.log(10.0)
    row_scale = jnp.exp(jax.random.uniform(jax.random.fold_in(key, 21), (TOKENS, 1), jnp.float32, 0.0, spread)) / math.sqrt(10.0)
    col_scale = jnp.exp(jax.random.uniform(jax.random.fold_in(key, 22), (1, FF), jnp.float32, 0.0, spread)) / math.sqrt(10.0)
    noise_field = jnp.clip(jax.random.normal(jax.random.fold_in(key, 23), (TOKENS, FF), jnp.float32), -6.0, 6.0)
    drawn_feats = 0.5 * noise_field * row_scale * col_scale
    return drawn_feats.astype(jnp.bfloat16)


def draw_keep_tiles(key, part):
    positions = jnp.arange(TOKENS, dtype=jnp.int32)
    threshold = 250 + 500 * positions // max(TOKENS - 1, 1)
    rolled = jax.random.randint(jax.random.fold_in(key, 31), (TOKENS, FF // TILE), 0, 1000, dtype=jnp.int32)
    keep_drawn = (rolled < threshold[:, None]).astype(jnp.int32)
    return keep_drawn.at[0].set(1)


def draw_band_span(key, part):
    spans_drawn = jax.random.randint(jax.random.fold_in(key, 41), (TOKENS,), WINDOW // 4, WINDOW + 1, dtype=jnp.int32)
    return spans_drawn.at[TOKENS - 1].set(WINDOW)


def shard_levels(own_key, dims, cuts, smallest, high):
    gain = 1.0
    for axis_at, shards_of in cuts:
        draws = jax.random.uniform(jax.random.fold_in(jax.random.fold_in(own_key, 6), axis_at), (shards_of,), jnp.float32, smallest / len(cuts), high / len(cuts))
        gain = gain * jnp.repeat(jnp.exp(draws), dims[axis_at] // shards_of).reshape((-1,) + (1,) * (len(dims) - 1 - axis_at))
    return gain


def bell_draw(key, dims, width, reach, shards=(), kind=jnp.bfloat16):
    factor_of = shard_levels(key, dims, shards, -0.22, 0.18) if shards else 1.0
    drawn = jax.random.normal(key, dims, jnp.float32) * width * factor_of
    return jnp.minimum(jnp.maximum(drawn, -reach), reach).astype(kind)


def setup_inputs(seed: int = 0, part: int = 0) -> dict:
    key_list = jax.random.split(jax.random.key(seed), 12)
    own_keys = jax.random.split(jax.random.fold_in(key_list[11], part), 12)
    return {
        "student_query": draw_student_query(jax.random.fold_in(jax.random.fold_in(key_list[11], part), 71), part),
        "teacher_keys": draw_teacher_keys(jax.random.fold_in(jax.random.fold_in(key_list[11], part), 71), part),
        "teacher_values": bell_draw(own_keys[2], (TOKENS, KV_HEADS * HEAD_DIM), 1.0, 6.0, ((0, 4), (1, 4))),
        "band_span": draw_band_span(jax.random.fold_in(jax.random.fold_in(key_list[11], part), 71), part),
        "residual_in": bell_draw(own_keys[4], (TOKENS, D), 0.5, 3.0, ((0, 4), (1, 4))),
        "norm_gain": jnp.clip(1.0 + 0.15 * jax.random.normal(key_list[5], (D,), jnp.float32), 0.25, 1.75),
        "w_gate": bell_draw(key_list[6], (D, FF), D ** -0.5, 0.09375, ((0, 4), (1, 4))),
        "w_up": bell_draw(key_list[7], (D, FF), D ** -0.5, 0.09375, ((0, 4), (1, 4))),
        "w_down": bell_draw(key_list[8], (FF, D), FF ** -0.5, 0.0625, ((0, 4), (1, 4))),
        "teacher_feats": draw_teacher_feats(jax.random.fold_in(jax.random.fold_in(key_list[11], part), 71), part),
        "keep_tiles": draw_keep_tiles(jax.random.fold_in(jax.random.fold_in(key_list[11], part), 71), part),
    }


def reference(student_query, teacher_keys, teacher_values, band_span, residual_in, norm_gain, w_gate, w_up, w_down, teacher_feats, keep_tiles):
    group_size = HEADS // KV_HEADS
    query_block = math.gcd(TOKENS, 512)
    span_length = WINDOW + query_block
    keys_padded = jnp.pad(teacher_keys, ((WINDOW, 0), (0, 0)))
    values_padded = jnp.pad(teacher_values, ((WINDOW, 0), (0, 0)))
    score_scale = 1.0 / math.sqrt(HEAD_DIM)

    def one_block(block_index):
        first_row = block_index * query_block
        query_rows = lax.dynamic_slice_in_dim(student_query, first_row, query_block, 0)
        query_rows = query_rows.astype(jnp.float32).reshape(query_block, KV_HEADS, group_size, HEAD_DIM)
        key_rows = lax.dynamic_slice_in_dim(keys_padded, first_row, span_length, 0)
        key_rows = key_rows.astype(jnp.float32).reshape(span_length, KV_HEADS, HEAD_DIM)
        value_rows = lax.dynamic_slice_in_dim(values_padded, first_row, span_length, 0)
        value_rows = value_rows.astype(jnp.float32).reshape(span_length, KV_HEADS, HEAD_DIM)
        spans_here = lax.dynamic_slice_in_dim(band_span, first_row, query_block, 0)
        query_pos = first_row + jnp.arange(query_block, dtype=jnp.int32)
        key_pos = first_row - WINDOW + jnp.arange(span_length, dtype=jnp.int32)
        distance = query_pos[:, None] - key_pos[None, :]
        allowed = (distance >= 0) & (distance < spans_here[:, None]) & (key_pos[None, :] >= 0)
        scores = jnp.einsum('tkgd,skd->kgts', query_rows, key_rows) * score_scale
        masked = jnp.where(allowed[None, None], scores, -jnp.inf)
        highest = lax.optimization_barrier(jnp.max(masked, axis=-1, keepdims=True))
        weights = jnp.exp(masked - highest)
        normalized = (weights / lax.optimization_barrier(jnp.sum(weights, axis=-1, keepdims=True))).astype(jnp.bfloat16)
        mixed_rows = jnp.einsum('kgts,skd->tkgd', normalized.astype(jnp.float32), value_rows)
        return mixed_rows.reshape(query_block, D)
    attended = lax.map(one_block, jnp.arange(TOKENS // query_block, dtype=jnp.int32)).reshape(TOKENS, D)
    resid = (residual_in.astype(jnp.float32) + attended).astype(jnp.bfloat16)
    resid_float = resid.astype(jnp.float32)
    rms_value = jnp.sqrt(lax.optimization_barrier(jnp.mean(resid_float * resid_float, axis=1, keepdims=True)) + 1e-05)
    normed = (resid_float / rms_value * norm_gain).astype(jnp.bfloat16)
    gate_proj = jnp.dot(normed, w_gate, preferred_element_type=jnp.float32)
    up_proj = jnp.dot(normed, w_up, preferred_element_type=jnp.float32)
    lifted = jnp.maximum(gate_proj, 0.0)
    squared = lifted * lifted
    act_value = squared * up_proj
    hidden = act_value.astype(jnp.bfloat16)
    summed_out = resid_float
    for group_index in range(FF // GROUP_FF):
        first_col = group_index * GROUP_FF
        last_col = first_col + GROUP_FF
        group_term = jnp.dot(hidden[:, first_col:last_col], w_down[first_col:last_col, :], preferred_element_type=jnp.float32)
        summed_out = summed_out + group_term.astype(jnp.bfloat16).astype(jnp.float32)
    layer_out = summed_out.astype(jnp.bfloat16)
    keep_wide = jnp.repeat(keep_tiles.astype(jnp.float32), TILE, axis=1)
    differ = act_value - teacher_feats.astype(jnp.float32)
    kept_total = jnp.sum(keep_tiles.astype(jnp.float32)) * TILE
    loss_value = (jnp.sum(keep_wide * differ * differ) / kept_total).reshape(1)
    grad_act = keep_wide * differ
    grad_gate = (grad_act * up_proj * 2.0 * lifted).astype(jnp.bfloat16)
    grad_up = (grad_act * squared).astype(jnp.bfloat16)
    grad_norm = jnp.zeros((TOKENS, D), jnp.float32)
    for group_index in range(FF // GROUP_FF):
        first_col = group_index * GROUP_FF
        last_col = first_col + GROUP_FF
        group_term = jnp.dot(grad_gate[:, first_col:last_col], w_gate[:, first_col:last_col].T, preferred_element_type=jnp.float32)
        group_term = group_term + jnp.dot(grad_up[:, first_col:last_col], w_up[:, first_col:last_col].T, preferred_element_type=jnp.float32)
        grad_norm = grad_norm + group_term.astype(jnp.bfloat16).astype(jnp.float32)
    inner_sum = lax.optimization_barrier(jnp.sum(norm_gain * grad_norm * resid_float, axis=1, keepdims=True))
    grad_resid = norm_gain * grad_norm / rms_value - resid_float * inner_sum / (D * rms_value * rms_value * rms_value)
    return (layer_out, loss_value, grad_resid)
```

```python
import math

import jax
import jax.numpy as jnp
from jax import lax
from jax.sharding import PartitionSpec as P

D = 4096
HEADS = 32
KV_HEADS = 8
HEAD_DIM = 128
TILE = 128
WINDOW = 1024
HP = ("head", "pair")
F32 = jnp.float32
BF16 = jnp.bfloat16


def passed_along(block, axis, distance):
    devices = range(lax.axis_size(axis))
    route = [(i - distance, i) for i in devices if i - distance in devices]
    return lax.ppermute(block, axis, route)


def swapped(block, axis):
    return lax.ppermute(block, axis, [(0, 1), (1, 0)])


def transposed(block):
    n = lax.axis_size("ctx")
    route = [(c * n + h, h * n + c) for c in range(n) for h in range(n)]
    return lax.ppermute(block, ("ctx",) + HP, route)


def attend_heads(query_part, key_rows, value_rows, allowed):
    scores = jnp.einsum("thd,sd->hts", query_part, key_rows, preferred_element_type=F32) * (
        1.0 / math.sqrt(HEAD_DIM)
    )
    masked = jnp.where(allowed[None], scores, -jnp.inf)
    highest = jnp.max(masked, axis=-1, keepdims=True)
    weights = jnp.exp(masked - highest)
    normalized = (weights / jnp.sum(weights, axis=-1, keepdims=True)).astype(BF16)
    return jnp.einsum("hts,sd->thd", normalized, value_rows, preferred_element_type=F32)


def attention(student_query, teacher_keys, teacher_values, band_span):
    rows = student_query.shape[0]
    kv_local = teacher_keys.shape[1] // HEAD_DIM
    group_size = HEADS // KV_HEADS
    ctx_index = lax.axis_index("ctx")
    paired = jnp.stack([teacher_keys, teacher_values])
    back = min(-(-WINDOW // rows), lax.axis_size("ctx") - 1)
    blocks = [paired] + [passed_along(paired, "ctx", d) for d in range(1, back + 1)]
    round_ids = jnp.arange(back + 1, dtype=jnp.int32)
    key_pos = (
        (ctx_index - round_ids)[:, None] * rows + jnp.arange(rows, dtype=jnp.int32)[None, :]
    ).reshape(-1)
    query_pos = ctx_index * rows + jnp.arange(rows, dtype=jnp.int32)
    distance = query_pos[:, None] - key_pos[None, :]
    allowed = (distance >= 0) & (distance < band_span[:, None]) & (key_pos[None, :] >= 0)
    all_blocks = jnp.concatenate(blocks, axis=1)
    outputs = []
    for kv_head in range(kv_local):
        cols = slice(kv_head * HEAD_DIM, (kv_head + 1) * HEAD_DIM)
        first = kv_head * group_size * HEAD_DIM
        query_part = student_query[:, first : first + group_size * HEAD_DIM]
        outputs.append(
            attend_heads(
                query_part.reshape(rows, group_size, HEAD_DIM),
                all_blocks[0][:, cols],
                all_blocks[1][:, cols],
                allowed,
            ).reshape(rows, group_size * HEAD_DIM)
        )
    return jnp.concatenate(outputs, axis=1)


def shifted(block, distance):
    return passed_along(block, "ctx", distance)


def picked(blocks, index):
    return lax.dynamic_index_in_dim(blocks, index, 0, keepdims=False)


def summed_over_hp(small):
    small = small + swapped(small, "pair")
    return small + swapped(small, "head")


def split_bits(wide):
    high = lax.reduce_precision(wide, 8, 7)
    middle = lax.reduce_precision(wide - high, 8, 7)
    return [v.astype(BF16) for v in (high, middle, wide - high - middle)]


def block_terms(gate_proj, up_proj, feats, keep_cols, weights):
    w_gate, w_up, w_down = weights
    rows, ff = gate_proj.shape
    tiles = keep_cols.shape[1]
    keep = jnp.broadcast_to(keep_cols.astype(F32)[:, :, None], (rows, tiles, TILE)).reshape(rows, ff)
    lifted = jnp.maximum(gate_proj, 0.0)
    squared = lifted * lifted
    act = squared * up_proj
    differ = act - feats.astype(F32)
    grad_act = keep * differ
    grad_gate = (grad_act * up_proj * 2.0 * lifted).astype(BF16)
    grad_up = (grad_act * squared).astype(BF16)
    contract = (((1,), (1,)), ((), ()))
    down = jnp.dot(act.astype(BF16), w_down, preferred_element_type=F32)
    grad = lax.dot_general(grad_gate, w_gate, contract, preferred_element_type=F32)
    grad = grad + lax.dot_general(grad_up, w_up, contract, preferred_element_type=F32)
    return down, grad, jnp.sum(grad_act * act, axis=1), jnp.sum(grad_act * differ)


def on_square(residual, norm_gain, weights, teacher_feats, keep_tiles):
    w_gate, w_up, _ = weights
    rows, d_ctx = residual.shape
    ff = w_gate.shape[1]
    tiles = keep_tiles.shape[1]
    z = lax.axis_index("ctx")
    hp = lax.axis_index(HP)
    low = z < 2

    tile = transposed(residual)
    own_wide = residual.astype(F32)
    mean = summed_over_hp(jnp.sum(own_wide * own_wide, axis=1)) / D
    rms = jnp.sqrt(mean + 1e-05)
    extra = [keep_tiles.astype(BF16)] + [v[:, None] for v in split_bits(rms)]
    marked = jnp.concatenate([teacher_feats] + extra, axis=1)
    marked = jnp.pad(marked, ((0, 0), (0, -marked.shape[1] % 128)))
    across = swapped(tile, "head")
    both = swapped(jnp.stack([tile, across]), "pair")
    marked, _ = lax.optimization_barrier((marked, tile))
    mark_right, mark_left = [shifted(marked, 1)], [shifted(marked, -1)]

    gain = lax.dynamic_slice_in_dim(norm_gain, z * d_ctx, d_ctx, 0)
    resid = jnp.stack([tile, both[0], across, both[1]]).astype(F32)
    scaled = (resid * gain).astype(BF16).reshape(4 * rows, d_ctx)
    parts = [
        jnp.dot(scaled, w, preferred_element_type=F32).astype(BF16).reshape(4, rows, ff)
        for w in (w_gate, w_up)
    ]

    came = [[None, None], [None, None]]
    for s in range(3):
        if s == 1:
            held, _ = lax.optimization_barrier(((mark_right[0], mark_left[0]), came[0][0]))
            mark_right.append(shifted(held[0], 1))
            mark_left.append(shifted(held[1], -1))
        if s == 2:
            held, _ = lax.optimization_barrier(((mark_right[1], mark_left[1]), came[0][0]))
            mark_right.append(shifted(held[0], 1))
            mark_left.append(shifted(held[1], -1))
        for i in range(2):
            right = picked(parts[i], jnp.clip(3 - s + z, 0, 3) ^ hp)
            left = picked(parts[i], jnp.clip(s - 3 + z, 0, 3) ^ hp)
            if s > 0:
                right = (right.astype(F32) + came[i][0].astype(F32)).astype(BF16)
                left = (left.astype(F32) + came[i][1].astype(F32)).astype(BF16)
            came[i] = [shifted(right, 1), shifted(left, -1)]
    owned = jnp.concatenate(
        [
            (picked(parts[i], z ^ hp).astype(F32) + came[i][0].astype(F32) + came[i][1].astype(F32)).astype(BF16)
            for i in range(2)
        ],
        axis=1,
    )

    owned, mark_right[2], mark_left[2] = lax.optimization_barrier((owned, mark_right[2], mark_left[2]))
    right, left = [shifted(owned, 1)], [shifted(owned, -1)]
    for s in range(2):
        right.append(shifted(right[s], 1))
        left.append(shifted(left[s], -1))

    def slots_of(mine, right, left):
        first = jnp.where(low, left[0], right[0])
        second = jnp.where(low, left[1], right[1])
        inner = jnp.where(low, right[0], left[0])
        outer = jnp.where(low, left[2], right[2])
        third = jnp.where((z == 0) | (z == 3), outer, inner)
        return [mine, first, second, third]

    def slot(token):
        return jnp.where(low, token - z, z - token) & 3

    sums = slots_of(owned, right, left)
    marks = slots_of(marked, mark_right, mark_left)
    results, rms_slots = [], []
    for k in range(4):
        bits = marks[k][:, ff + tiles : ff + tiles + 3].astype(F32)
        rms_k = bits[:, 0] + bits[:, 1] + bits[:, 2]
        inv = (1.0 / rms_k)[:, None]
        rms_slots.append(rms_k)
        results.append(
            block_terms(
                sums[k][:, :ff].astype(F32) * inv,
                sums[k][:, ff:].astype(F32) * inv,
                marks[k][:, :ff],
                marks[k][:, ff : ff + tiles],
                weights,
            )
        )
    down, grad, inner, loss = [[r[i] for r in results] for i in range(4)]

    count = sum(jnp.sum(m[:, ff : ff + tiles].astype(F32)) for m in marks) * TILE
    inner = jnp.stack(inner)
    by_token = jnp.concatenate([picked(inner, slot(t)) for t in range(4)])
    small = jnp.concatenate([by_token, sum(loss)[None], count[None], jnp.zeros(126, F32)])
    small = summed_over_hp(small)
    loss_value = (small[4 * rows] / small[4 * rows + 1]).reshape(1)
    rms_own = picked(jnp.stack(rms_slots), slot(hp))[:, None]
    inner_own = 3.0 * rms_own * lax.dynamic_slice_in_dim(small, hp * rows, rows, 0)[:, None]

    def reduced(blocks):
        blocks = jnp.stack(blocks)
        j = [picked(blocks, slot(i ^ hp)) for i in range(4)]
        came = swapped(jnp.stack([j[1], j[3]]).astype(BF16), "pair").astype(F32)
        half = (j[2] + came[1]).astype(BF16)
        return j[0] + came[0] + swapped(half, "head").astype(F32)

    own = tile.astype(F32)
    layer_out = transposed((own + reduced(down)).astype(BF16))
    slope = gain * reduced(grad) / rms_own - own * inner_own / (D * rms_own * rms_own * rms_own)
    return layer_out, loss_value, transposed(slope.astype(BF16)).astype(F32)


def on_any(residual, norm_gain, weights, teacher_feats, keep_tiles):
    w_gate, w_up, _ = weights
    rows = residual.shape[0]
    d_ctx, ff = w_gate.shape
    tiles = keep_tiles.shape[1]
    n_ctx = lax.axis_size("ctx")
    z = lax.axis_index("ctx")
    hp = lax.axis_index(HP)
    keep_cols = jnp.pad(keep_tiles.astype(BF16), ((0, 0), (0, -tiles % 128)))
    marked = lax.all_gather(jnp.concatenate([teacher_feats, keep_cols], axis=1), "ctx", tiled=True)
    wide = lax.all_gather(residual, HP, axis=1, tiled=True)
    resid = lax.all_to_all(wide, "ctx", split_axis=1, concat_axis=0, tiled=True).astype(F32)
    gain = lax.dynamic_slice_in_dim(norm_gain, z * d_ctx, d_ctx, 0)
    rms = jnp.sqrt(lax.psum(jnp.sum(resid * resid, axis=1), "ctx") / D + 1e-05)
    scaled = (resid * gain).astype(BF16)
    inv = (1.0 / rms)[:, None]
    sums = [
        lax.psum(jnp.dot(scaled, w, preferred_element_type=F32).astype(BF16), "ctx").astype(F32) * inv
        for w in (w_gate, w_up)
    ]
    keep_cols = marked[:, ff : ff + tiles]
    down, grad, inner, loss = block_terms(sums[0], sums[1], marked[:, :ff], keep_cols, weights)
    count = jnp.sum(keep_cols.astype(F32)) * TILE
    small = lax.psum(jnp.concatenate([inner, loss[None], count[None]]), HP)
    loss_value = (small[-2] / small[-1]).reshape(1)

    def home(whole):
        routed = lax.all_to_all(whole.astype(BF16), "ctx", 0, 1, tiled=True)
        return lax.psum_scatter(routed, HP, scatter_dimension=1, tiled=True).astype(F32)

    own = residual.astype(F32)
    layer_out = (own + home(down)).astype(BF16)
    rms_own = lax.dynamic_slice_in_dim(rms, z * rows, rows, 0)[:, None]
    inner_own = 3.0 * rms_own * lax.dynamic_slice_in_dim(small, z * rows, rows, 0)[:, None]
    gain_own = lax.dynamic_slice_in_dim(norm_gain, hp * own.shape[1], own.shape[1], 0)
    slope = gain_own * home(grad) / rms_own - own * inner_own / (D * rms_own * rms_own * rms_own)
    return layer_out, loss_value, slope


def local(
    student_query,
    teacher_keys,
    teacher_values,
    band_span,
    residual_in,
    norm_gain,
    w_gate,
    w_up,
    w_down,
    teacher_feats,
    keep_tiles,
):
    attended = attention(student_query, teacher_keys, teacher_values, band_span)
    residual = (residual_in.astype(F32) + attended).astype(BF16)
    sizes = tuple(lax.axis_size(a) for a in ("ctx", "head", "pair"))
    finish = on_square if sizes == (4, 2, 2) else on_any
    return finish(residual, norm_gain, (w_gate, w_up, w_down), teacher_feats, keep_tiles)


def solution(mesh):
    rows = P(("groups", "ctx"), HP)
    in_specs = (
        rows, rows, rows, P(("groups", "ctx")), rows, P(),
        P("ctx", HP), P("ctx", HP), P(HP, "ctx"), rows, rows,
    )
    out_specs = (rows, P("groups"), rows)
    return jax.shard_map(local, mesh=mesh, in_specs=in_specs, out_specs=out_specs, check_vma=False)
```

```python
import math

import jax
import jax.numpy as jnp
from jax import lax
from jax.experimental.layout import Layout, with_layout_constraint
from jax.sharding import PartitionSpec as P

D = 4096
HEADS = 32
KV_HEADS = 8
HEAD_DIM = 128
TILE = 128
WINDOW = 1024
HP = ("head", "pair")
F32 = jnp.float32
BF16 = jnp.bfloat16


def passed_along(block, axis, distance):
    devices = range(lax.axis_size(axis))
    route = [(i - distance, i) for i in devices if i - distance in devices]
    return lax.ppermute(block, axis, route)


def swapped(block, axis):
    return lax.ppermute(block, axis, [(0, 1), (1, 0)])


def transposed(block):
    n = lax.axis_size("ctx")
    route = [(c * n + h, h * n + c) for c in range(n) for h in range(n)]
    return lax.ppermute(block, ("ctx",) + HP, route)


def attend_heads(query_part, key_rows, value_rows, allowed):
    scores = jnp.einsum("thd,sd->hts", query_part, key_rows, preferred_element_type=F32) * (
        1.0 / math.sqrt(HEAD_DIM)
    )
    masked = jnp.where(allowed[None], scores, -jnp.inf)
    highest = jnp.max(masked, axis=-1, keepdims=True)
    weights = jnp.exp(masked - highest)
    normalized = (weights / jnp.sum(weights, axis=-1, keepdims=True)).astype(BF16)
    return jnp.einsum("hts,sd->thd", normalized, value_rows, preferred_element_type=F32)


def attention(student_query, teacher_keys, teacher_values, band_span):
    rows = student_query.shape[0]
    kv_local = teacher_keys.shape[1] // HEAD_DIM
    group_size = HEADS // KV_HEADS
    ctx_index = lax.axis_index("ctx")
    paired = jnp.stack([teacher_keys, teacher_values])
    back = min(-(-WINDOW // rows), lax.axis_size("ctx") - 1)
    blocks = [paired] + [passed_along(paired, "ctx", d) for d in range(1, back + 1)]
    round_ids = jnp.arange(back + 1, dtype=jnp.int32)
    key_pos = (
        (ctx_index - round_ids)[:, None] * rows + jnp.arange(rows, dtype=jnp.int32)[None, :]
    ).reshape(-1)
    query_pos = ctx_index * rows + jnp.arange(rows, dtype=jnp.int32)
    distance = query_pos[:, None] - key_pos[None, :]
    allowed = (distance >= 0) & (distance < band_span[:, None]) & (key_pos[None, :] >= 0)
    all_blocks = jnp.concatenate(blocks, axis=1)
    outputs = []
    for kv_head in range(kv_local):
        cols = slice(kv_head * HEAD_DIM, (kv_head + 1) * HEAD_DIM)
        first = kv_head * group_size * HEAD_DIM
        query_part = student_query[:, first : first + group_size * HEAD_DIM]
        outputs.append(
            attend_heads(
                query_part.reshape(rows, group_size, HEAD_DIM),
                all_blocks[0][:, cols],
                all_blocks[1][:, cols],
                allowed,
            ).reshape(rows, group_size * HEAD_DIM)
        )
    return jnp.concatenate(outputs, axis=1)


def row_major(block):
    return with_layout_constraint(block, Layout(major_to_minor=tuple(range(block.ndim))))


def shifted(block, distance):
    return row_major(passed_along(row_major(block), "ctx", distance))


def picked(blocks, index):
    return lax.dynamic_index_in_dim(blocks, index, 0, keepdims=False)


def summed_over_hp(small):
    small = small + swapped(small, "pair")
    return small + swapped(small, "head")


def split_bits(wide):
    high = lax.reduce_precision(wide, 8, 7)
    middle = lax.reduce_precision(wide - high, 8, 7)
    return [v.astype(BF16) for v in (high, middle, wide - high - middle)]


def block_terms(gate_proj, up_proj, feats, keep_cols, weights):
    w_gate, w_up, w_down = weights
    rows, ff = gate_proj.shape
    tiles = keep_cols.shape[1]
    keep = jnp.broadcast_to(keep_cols.astype(F32)[:, :, None], (rows, tiles, TILE)).reshape(rows, ff)
    lifted = jnp.maximum(gate_proj, 0.0)
    squared = lifted * lifted
    act = squared * up_proj
    differ = act - feats.astype(F32)
    grad_act = keep * differ
    grad_gate = (grad_act * up_proj * 2.0 * lifted).astype(BF16)
    grad_up = (grad_act * squared).astype(BF16)
    contract = (((1,), (1,)), ((), ()))
    down = jnp.dot(act.astype(BF16), w_down, preferred_element_type=F32)
    grad = lax.dot_general(grad_gate, w_gate, contract, preferred_element_type=F32)
    grad = grad + lax.dot_general(grad_up, w_up, contract, preferred_element_type=F32)
    return down, grad, jnp.sum(grad_act * act, axis=1), jnp.sum(grad_act * differ)


def on_square(residual, norm_gain, weights, teacher_feats, keep_tiles):
    w_gate, w_up, _ = weights
    rows, d_ctx = residual.shape
    ff = w_gate.shape[1]
    tiles = keep_tiles.shape[1]
    z = lax.axis_index("ctx")
    hp = lax.axis_index(HP)
    low = z < 2

    tile = transposed(residual)
    own_wide = residual.astype(F32)
    mean = summed_over_hp(jnp.sum(own_wide * own_wide, axis=1)) / D
    rms = jnp.sqrt(mean + 1e-05)
    extra = [keep_tiles.astype(BF16)] + [v[:, None] for v in split_bits(rms)]
    marked = jnp.concatenate([teacher_feats] + extra, axis=1)
    marked = jnp.pad(marked, ((0, 0), (0, -marked.shape[1] % 128)))
    across = swapped(tile, "head")
    both = swapped(jnp.stack([tile, across]), "pair")
    marked, _ = lax.optimization_barrier((marked, tile))
    mark_right, mark_left = [shifted(marked, 1)], [shifted(marked, -1)]

    gain = lax.dynamic_slice_in_dim(norm_gain, z * d_ctx, d_ctx, 0)
    resid = jnp.stack([tile, both[0], across, both[1]]).astype(F32)
    scaled = (resid * gain).astype(BF16).reshape(4 * rows, d_ctx)
    parts = [
        jnp.dot(scaled, w, preferred_element_type=F32).astype(BF16).reshape(4, rows, ff)
        for w in (w_gate, w_up)
    ]

    came = [[None, None], [None, None]]
    for s in range(3):
        if s == 1:
            held, _ = lax.optimization_barrier(((mark_right[0], mark_left[0]), came[0][0]))
            mark_right.append(shifted(held[0], 1))
            mark_left.append(shifted(held[1], -1))
        if s == 2:
            held, _ = lax.optimization_barrier(((mark_right[1], mark_left[1]), came[0][0]))
            mark_right.append(shifted(held[0], 1))
            mark_left.append(shifted(held[1], -1))
        for i in range(2):
            right = picked(parts[i], jnp.clip(3 - s + z, 0, 3) ^ hp)
            left = picked(parts[i], jnp.clip(s - 3 + z, 0, 3) ^ hp)
            if s > 0:
                right = (right.astype(F32) + came[i][0].astype(F32)).astype(BF16)
                left = (left.astype(F32) + came[i][1].astype(F32)).astype(BF16)
            came[i] = [shifted(right, 1), shifted(left, -1)]
    owned = jnp.concatenate(
        [
            (picked(parts[i], z ^ hp).astype(F32) + came[i][0].astype(F32) + came[i][1].astype(F32)).astype(BF16)
            for i in range(2)
        ],
        axis=1,
    )

    owned, mark_right[2], mark_left[2] = lax.optimization_barrier((owned, mark_right[2], mark_left[2]))
    right, left = [shifted(owned, 1)], [shifted(owned, -1)]
    for s in range(2):
        right.append(shifted(right[s], 1))
        left.append(shifted(left[s], -1))

    def slots_of(mine, right, left):
        first = jnp.where(low, left[0], right[0])
        second = jnp.where(low, left[1], right[1])
        inner = jnp.where(low, right[0], left[0])
        outer = jnp.where(low, left[2], right[2])
        third = jnp.where((z == 0) | (z == 3), outer, inner)
        return [mine, first, second, third]

    def slot(token):
        return jnp.where(low, token - z, z - token) & 3

    sums = slots_of(owned, right, left)
    marks = slots_of(marked, mark_right, mark_left)
    results, rms_slots = [], []
    for k in range(4):
        bits = marks[k][:, ff + tiles : ff + tiles + 3].astype(F32)
        rms_k = bits[:, 0] + bits[:, 1] + bits[:, 2]
        inv = (1.0 / rms_k)[:, None]
        rms_slots.append(rms_k)
        results.append(
            block_terms(
                sums[k][:, :ff].astype(F32) * inv,
                sums[k][:, ff:].astype(F32) * inv,
                marks[k][:, :ff],
                marks[k][:, ff : ff + tiles],
                weights,
            )
        )
    down, grad, inner, loss = [[r[i] for r in results] for i in range(4)]

    count = sum(jnp.sum(m[:, ff : ff + tiles].astype(F32)) for m in marks) * TILE
    inner = jnp.stack(inner)
    by_token = jnp.concatenate([picked(inner, slot(t)) for t in range(4)])
    small = jnp.concatenate([by_token, sum(loss)[None], count[None], jnp.zeros(126, F32)])
    small = summed_over_hp(small)
    loss_value = (small[4 * rows] / small[4 * rows + 1]).reshape(1)
    rms_own = picked(jnp.stack(rms_slots), slot(hp))[:, None]
    inner_own = 3.0 * rms_own * lax.dynamic_slice_in_dim(small, hp * rows, rows, 0)[:, None]

    def reduced(blocks):
        blocks = jnp.stack(blocks)
        j = [picked(blocks, slot(i ^ hp)) for i in range(4)]
        came = swapped(jnp.stack([j[1], j[3]]).astype(BF16), "pair").astype(F32)
        half = (j[2] + came[1]).astype(BF16)
        return j[0] + came[0] + swapped(half, "head").astype(F32)

    own = tile.astype(F32)
    layer_out = transposed((own + reduced(down)).astype(BF16))
    slope = gain * reduced(grad) / rms_own - own * inner_own / (D * rms_own * rms_own * rms_own)
    return layer_out, loss_value, transposed(slope.astype(BF16)).astype(F32)


def on_any(residual, norm_gain, weights, teacher_feats, keep_tiles):
    w_gate, w_up, _ = weights
    rows = residual.shape[0]
    d_ctx, ff = w_gate.shape
    tiles = keep_tiles.shape[1]
    n_ctx = lax.axis_size("ctx")
    z = lax.axis_index("ctx")
    hp = lax.axis_index(HP)
    keep_cols = jnp.pad(keep_tiles.astype(BF16), ((0, 0), (0, -tiles % 128)))
    marked = lax.all_gather(jnp.concatenate([teacher_feats, keep_cols], axis=1), "ctx", tiled=True)
    wide = lax.all_gather(residual, HP, axis=1, tiled=True)
    resid = lax.all_to_all(wide, "ctx", split_axis=1, concat_axis=0, tiled=True).astype(F32)
    gain = lax.dynamic_slice_in_dim(norm_gain, z * d_ctx, d_ctx, 0)
    rms = jnp.sqrt(lax.psum(jnp.sum(resid * resid, axis=1), "ctx") / D + 1e-05)
    scaled = (resid * gain).astype(BF16)
    inv = (1.0 / rms)[:, None]
    sums = [
        lax.psum(jnp.dot(scaled, w, preferred_element_type=F32).astype(BF16), "ctx").astype(F32) * inv
        for w in (w_gate, w_up)
    ]
    keep_cols = marked[:, ff : ff + tiles]
    down, grad, inner, loss = block_terms(sums[0], sums[1], marked[:, :ff], keep_cols, weights)
    count = jnp.sum(keep_cols.astype(F32)) * TILE
    small = lax.psum(jnp.concatenate([inner, loss[None], count[None]]), HP)
    loss_value = (small[-2] / small[-1]).reshape(1)

    def home(whole):
        routed = lax.all_to_all(whole.astype(BF16), "ctx", 0, 1, tiled=True)
        return lax.psum_scatter(routed, HP, scatter_dimension=1, tiled=True).astype(F32)

    own = residual.astype(F32)
    layer_out = (own + home(down)).astype(BF16)
    rms_own = lax.dynamic_slice_in_dim(rms, z * rows, rows, 0)[:, None]
    inner_own = 3.0 * rms_own * lax.dynamic_slice_in_dim(small, z * rows, rows, 0)[:, None]
    gain_own = lax.dynamic_slice_in_dim(norm_gain, hp * own.shape[1], own.shape[1], 0)
    slope = gain_own * home(grad) / rms_own - own * inner_own / (D * rms_own * rms_own * rms_own)
    return layer_out, loss_value, slope


def local(
    student_query,
    teacher_keys,
    teacher_values,
    band_span,
    residual_in,
    norm_gain,
    w_gate,
    w_up,
    w_down,
    teacher_feats,
    keep_tiles,
):
    attended = attention(student_query, teacher_keys, teacher_values, band_span)
    residual = (residual_in.astype(F32) + attended).astype(BF16)
    sizes = tuple(lax.axis_size(a) for a in ("ctx", "head", "pair"))
    finish = on_square if sizes == (4, 2, 2) else on_any
    return finish(residual, norm_gain, (w_gate, w_up, w_down), teacher_feats, keep_tiles)


def solution(mesh):
    rows = P(("groups", "ctx"), HP)
    in_specs = (
        rows, rows, rows, P(("groups", "ctx")), rows, P(),
        P("ctx", HP), P("ctx", HP), P(HP, "ctx"), rows, rows,
    )
    out_specs = (rows, P("groups"), rows)
    return jax.shard_map(local, mesh=mesh, in_specs=in_specs, out_specs=out_specs, check_vma=False)
```

```python
import math

import jax
import jax.numpy as jnp
from jax import lax
from jax.experimental.layout import Layout, with_layout_constraint
from jax.sharding import PartitionSpec as P

D = 4096
HEADS = 32
KV_HEADS = 8
HEAD_DIM = 128
TILE = 128
WINDOW = 1024
HP = ("head", "pair")
F32 = jnp.float32
BF16 = jnp.bfloat16


def passed_along(block, axis, distance):
    devices = range(lax.axis_size(axis))
    route = [(i - distance, i) for i in devices if i - distance in devices]
    return lax.ppermute(block, axis, route)


def swapped(block, axis):
    return lax.ppermute(block, axis, [(0, 1), (1, 0)])


def transposed(block):
    n = lax.axis_size("ctx")
    route = [(c * n + h, h * n + c) for c in range(n) for h in range(n)]
    return lax.ppermute(block, ("ctx",) + HP, route)


def attend_heads(query_part, key_rows, value_rows, allowed):
    scores = jnp.einsum("thd,sd->hts", query_part, key_rows, preferred_element_type=F32) * (
        1.0 / math.sqrt(HEAD_DIM)
    )
    masked = jnp.where(allowed[None], scores, -jnp.inf)
    highest = jnp.max(masked, axis=-1, keepdims=True)
    weights = jnp.exp(masked - highest)
    normalized = (weights / jnp.sum(weights, axis=-1, keepdims=True)).astype(BF16)
    return jnp.einsum("hts,sd->thd", normalized, value_rows, preferred_element_type=F32)


def attention(student_query, teacher_keys, teacher_values, band_span):
    rows = student_query.shape[0]
    kv_local = teacher_keys.shape[1] // HEAD_DIM
    group_size = HEADS // KV_HEADS
    ctx_index = lax.axis_index("ctx")
    paired = jnp.stack([teacher_keys, teacher_values])
    back = min(-(-WINDOW // rows), lax.axis_size("ctx") - 1)
    blocks = [paired] + [passed_along(paired, "ctx", d) for d in range(1, back + 1)]
    round_ids = jnp.arange(back + 1, dtype=jnp.int32)
    key_pos = (
        (ctx_index - round_ids)[:, None] * rows + jnp.arange(rows, dtype=jnp.int32)[None, :]
    ).reshape(-1)
    query_pos = ctx_index * rows + jnp.arange(rows, dtype=jnp.int32)
    distance = query_pos[:, None] - key_pos[None, :]
    allowed = (distance >= 0) & (distance < band_span[:, None]) & (key_pos[None, :] >= 0)
    all_blocks = jnp.concatenate(blocks, axis=1)
    outputs = []
    for kv_head in range(kv_local):
        cols = slice(kv_head * HEAD_DIM, (kv_head + 1) * HEAD_DIM)
        first = kv_head * group_size * HEAD_DIM
        query_part = student_query[:, first : first + group_size * HEAD_DIM]
        outputs.append(
            attend_heads(
                query_part.reshape(rows, group_size, HEAD_DIM),
                all_blocks[0][:, cols],
                all_blocks[1][:, cols],
                allowed,
            ).reshape(rows, group_size * HEAD_DIM)
        )
    return jnp.concatenate(outputs, axis=1)


def row_major(block):
    return with_layout_constraint(block, Layout(major_to_minor=tuple(range(block.ndim))))


def shifted(block, distance):
    return row_major(passed_along(row_major(block), "ctx", distance))


def picked(blocks, index):
    return lax.dynamic_index_in_dim(blocks, index, 0, keepdims=False)


def summed_over_hp(small):
    small = small + swapped(small, "pair")
    return small + swapped(small, "head")


def elementwise(gate_proj, up_proj, feats, keep_cols):
    rows, ff = gate_proj.shape
    tiles = keep_cols.shape[1]
    keep = jnp.broadcast_to(keep_cols.astype(F32)[:, :, None], (rows, tiles, TILE)).reshape(rows, ff)
    lifted = jnp.maximum(gate_proj, 0.0)
    squared = lifted * lifted
    act = squared * up_proj
    differ = act - feats.astype(F32)
    grad_act = keep * differ
    grad_gate = (grad_act * up_proj * 2.0 * lifted).astype(BF16)
    grad_up = (grad_act * squared).astype(BF16)
    inner = 3.0 * jnp.sum(grad_act * act, axis=1)
    return act.astype(BF16), grad_gate, grad_up, inner, jnp.sum(grad_act * differ)


def products(hidden, grad_gate, grad_up, weights):
    w_gate, w_up, w_down = weights
    contract = (((1,), (1,)), ((), ()))
    down = jnp.dot(hidden, w_down, preferred_element_type=F32)
    grad = lax.dot_general(grad_gate, w_gate, contract, preferred_element_type=F32)
    return down, grad + lax.dot_general(grad_up, w_up, contract, preferred_element_type=F32)


TURNS = ((0, 1, 2, 3), (1, 2, 3, 0), (2, 1, 0, 3), (3, 2, 1, 0))


def on_square(residual, norm_gain, weights, teacher_feats, keep_tiles):
    w_gate, w_up, _ = weights
    rows, d_ctx = residual.shape
    ff = w_gate.shape[1]
    z = lax.axis_index("ctx")
    hp = lax.axis_index(HP)
    pair = lax.axis_index("pair")
    low = z < 2

    tile = transposed(residual)
    own_wide = residual.astype(F32)
    mean = summed_over_hp(jnp.sum(own_wide * own_wide, axis=1)) / D
    rms = jnp.sqrt(mean + 1e-05)[:, None]
    across = swapped(tile, "head")
    both = swapped(jnp.stack([tile, across]), "pair")
    gain = lax.dynamic_slice_in_dim(norm_gain, z * d_ctx, d_ctx, 0)
    resid = jnp.stack([tile, both[0], across, both[1]]).astype(F32)
    scaled = (resid * gain).astype(BF16).reshape(4 * rows, d_ctx)
    parts = [
        jnp.dot(scaled, w, preferred_element_type=F32).astype(BF16).reshape(4, rows, ff)
        for w in (w_gate, w_up)
    ]

    came = [[None, None], [None, None]]
    for s in range(3):
        for i in range(2):
            right = picked(parts[i], jnp.clip(3 - s + z, 0, 3) ^ hp)
            left = picked(parts[i], jnp.clip(s - 3 + z, 0, 3) ^ hp)
            if s > 0:
                right = (right.astype(F32) + came[i][0].astype(F32)).astype(BF16)
                left = (left.astype(F32) + came[i][1].astype(F32)).astype(BF16)
            came[i] = [shifted(right, 1), shifted(left, -1)]
    gate_proj, up_proj = [
        (picked(parts[i], z ^ hp).astype(F32) + came[i][0].astype(F32) + came[i][1].astype(F32)) / rms
        for i in range(2)
    ]
    hidden, grad_gate, grad_up, inner, loss = elementwise(gate_proj, up_proj, teacher_feats, keep_tiles)
    owned = jnp.concatenate([hidden, grad_gate, grad_up], axis=1)

    right, left = [shifted(owned, 1)], [shifted(owned, -1)]
    for s in range(2):
        right.append(shifted(right[s], 1))
        left.append(shifted(left[s], -1))
    turns = [owned, jnp.where(low, left[0], right[0])]
    first, second = lax.optimization_barrier((turns[1], (left[1], right[1])))
    turns = [owned, first, jnp.where(low, *second)]
    second, third = lax.optimization_barrier((turns[2], (left[2], right[2])))
    outer = jnp.where(low, *third)
    inward = jnp.where(low, right[0], left[0])
    turns = [owned, first, second, jnp.where((z == 0) | (z == 3), outer, inward)]

    def brought_home(k, down, grad):
        keeps_down = pair == (k & 1)
        sent = jnp.where(keeps_down, grad, down).astype(BF16)
        half = jnp.where(keeps_down, down, grad) + swapped(sent, "pair").astype(F32)
        route = [(k ^ 2, k), (k ^ 1, k ^ 3)]
        whole = (half + lax.ppermute(half.astype(BF16), HP, route).astype(F32)).astype(BF16)
        return [
            lax.ppermute(whole, ("ctx",) + HP, [(4 * c + h, 4 * TURNS[c][k] + c) for c in range(4)])
            for h in (k, k ^ 3)
        ]

    home = []
    for k in range(4):
        block = turns[k]
        down, grad = products(block[:, :ff], block[:, ff : 2 * ff], block[:, 2 * ff :], weights)
        home.append(brought_home(k, down, grad))

    count = jnp.sum(keep_tiles.astype(F32)) * TILE
    small = jnp.concatenate([inner, loss[None], count[None], jnp.zeros(126, F32)])
    small = summed_over_hp(small)
    totals = small[rows:]
    for d in (1, 2):
        totals = totals + lax.ppermute(totals, "ctx", [(c, c ^ d) for c in range(4)])
    loss_value = (totals[0] / totals[1]).reshape(1)

    down, grad = [sum(h[i].astype(F32) for h in home) for i in range(2)]
    gain_own = lax.dynamic_slice_in_dim(norm_gain, hp * d_ctx, d_ctx, 0)
    layer_out = (own_wide + down).astype(BF16)
    inner_own = small[:rows][:, None] * rms
    slope = gain_own * grad / rms - own_wide * inner_own / (D * rms * rms * rms)
    return layer_out, loss_value, slope


def on_any(residual, norm_gain, weights, teacher_feats, keep_tiles):
    w_gate, w_up, _ = weights
    rows = residual.shape[0]
    d_ctx, ff = w_gate.shape
    tiles = keep_tiles.shape[1]
    n_ctx = lax.axis_size("ctx")
    z = lax.axis_index("ctx")
    hp = lax.axis_index(HP)
    keep_cols = jnp.pad(keep_tiles.astype(BF16), ((0, 0), (0, -tiles % 128)))
    marked = lax.all_gather(jnp.concatenate([teacher_feats, keep_cols], axis=1), "ctx", tiled=True)
    wide = lax.all_gather(residual, HP, axis=1, tiled=True)
    resid = lax.all_to_all(wide, "ctx", split_axis=1, concat_axis=0, tiled=True).astype(F32)
    gain = lax.dynamic_slice_in_dim(norm_gain, z * d_ctx, d_ctx, 0)
    rms = jnp.sqrt(lax.psum(jnp.sum(resid * resid, axis=1), "ctx") / D + 1e-05)
    scaled = (resid * gain).astype(BF16)
    inv = (1.0 / rms)[:, None]
    sums = [
        lax.psum(jnp.dot(scaled, w, preferred_element_type=F32).astype(BF16), "ctx").astype(F32) * inv
        for w in (w_gate, w_up)
    ]
    keep_cols = marked[:, ff : ff + tiles]
    *values, inner, loss = elementwise(sums[0], sums[1], marked[:, :ff], keep_cols)
    down, grad = products(*values, weights)
    count = jnp.sum(keep_cols.astype(F32)) * TILE
    small = lax.psum(jnp.concatenate([inner, loss[None], count[None]]), HP)
    loss_value = (small[-2] / small[-1]).reshape(1)

    def home(whole):
        routed = lax.all_to_all(whole.astype(BF16), "ctx", 0, 1, tiled=True)
        return lax.psum_scatter(routed, HP, scatter_dimension=1, tiled=True).astype(F32)

    own = residual.astype(F32)
    layer_out = (own + home(down)).astype(BF16)
    rms_own = lax.dynamic_slice_in_dim(rms, z * rows, rows, 0)[:, None]
    inner_own = rms_own * lax.dynamic_slice_in_dim(small, z * rows, rows, 0)[:, None]
    gain_own = lax.dynamic_slice_in_dim(norm_gain, hp * own.shape[1], own.shape[1], 0)
    slope = gain_own * home(grad) / rms_own - own * inner_own / (D * rms_own * rms_own * rms_own)
    return layer_out, loss_value, slope


def local(
    student_query,
    teacher_keys,
    teacher_values,
    band_span,
    residual_in,
    norm_gain,
    w_gate,
    w_up,
    w_down,
    teacher_feats,
    keep_tiles,
):
    attended = attention(student_query, teacher_keys, teacher_values, band_span)
    residual = (residual_in.astype(F32) + attended).astype(BF16)
    sizes = tuple(lax.axis_size(a) for a in ("ctx", "head", "pair"))
    finish = on_square if sizes == (4, 2, 2) else on_any
    return finish(residual, norm_gain, (w_gate, w_up, w_down), teacher_feats, keep_tiles)


def solution(mesh):
    rows = P(("groups", "ctx"), HP)
    in_specs = (
        rows, rows, rows, P(("groups", "ctx")), rows, P(),
        P("ctx", HP), P("ctx", HP), P(HP, "ctx"), rows, rows,
    )
    out_specs = (rows, P("groups"), rows)
    return jax.shard_map(local, mesh=mesh, in_specs=in_specs, out_specs=out_specs, check_vma=False)
```

```python
import math

import jax
import jax.numpy as jnp
from jax import lax
from jax.experimental.layout import Layout, with_layout_constraint
from jax.sharding import PartitionSpec as P

D = 4096
HEADS = 32
KV_HEADS = 8
HEAD_DIM = 128
TILE = 128
WINDOW = 1024
HP = ("head", "pair")
F32 = jnp.float32
BF16 = jnp.bfloat16


def passed_along(block, axis, distance):
    devices = range(lax.axis_size(axis))
    route = [(i - distance, i) for i in devices if i - distance in devices]
    return lax.ppermute(block, axis, route)


def swapped(block, axis):
    return lax.ppermute(block, axis, [(0, 1), (1, 0)])


def transposed(block):
    n = lax.axis_size("ctx")
    route = [(c * n + h, h * n + c) for c in range(n) for h in range(n)]
    return lax.ppermute(block, ("ctx",) + HP, route)


def attend_heads(query_part, key_rows, value_rows, allowed):
    scores = jnp.einsum("thd,sd->hts", query_part, key_rows, preferred_element_type=F32) * (
        1.0 / math.sqrt(HEAD_DIM)
    )
    masked = jnp.where(allowed[None], scores, -jnp.inf)
    highest = jnp.max(masked, axis=-1, keepdims=True)
    weights = jnp.exp(masked - highest)
    normalized = (weights / jnp.sum(weights, axis=-1, keepdims=True)).astype(BF16)
    return jnp.einsum("hts,sd->thd", normalized, value_rows, preferred_element_type=F32)


def attention(student_query, teacher_keys, teacher_values, band_span):
    rows = student_query.shape[0]
    kv_local = teacher_keys.shape[1] // HEAD_DIM
    group_size = HEADS // KV_HEADS
    ctx_index = lax.axis_index("ctx")
    paired = jnp.stack([teacher_keys, teacher_values])
    back = min(-(-WINDOW // rows), lax.axis_size("ctx") - 1)
    blocks = [paired] + [passed_along(paired, "ctx", d) for d in range(1, back + 1)]
    round_ids = jnp.arange(back + 1, dtype=jnp.int32)
    key_pos = (
        (ctx_index - round_ids)[:, None] * rows + jnp.arange(rows, dtype=jnp.int32)[None, :]
    ).reshape(-1)
    query_pos = ctx_index * rows + jnp.arange(rows, dtype=jnp.int32)
    distance = query_pos[:, None] - key_pos[None, :]
    allowed = (distance >= 0) & (distance < band_span[:, None]) & (key_pos[None, :] >= 0)
    all_blocks = jnp.concatenate(blocks, axis=1)
    outputs = []
    for kv_head in range(kv_local):
        cols = slice(kv_head * HEAD_DIM, (kv_head + 1) * HEAD_DIM)
        first = kv_head * group_size * HEAD_DIM
        query_part = student_query[:, first : first + group_size * HEAD_DIM]
        outputs.append(
            attend_heads(
                query_part.reshape(rows, group_size, HEAD_DIM),
                all_blocks[0][:, cols],
                all_blocks[1][:, cols],
                allowed,
            ).reshape(rows, group_size * HEAD_DIM)
        )
    return jnp.concatenate(outputs, axis=1)


def row_major(block):
    return with_layout_constraint(block, Layout(major_to_minor=tuple(range(block.ndim))))


def shifted(block, distance):
    return row_major(passed_along(row_major(block), "ctx", distance))


def picked(blocks, index):
    return lax.dynamic_index_in_dim(blocks, index, 0, keepdims=False)


def summed_over_hp(small):
    small = small + swapped(small, "pair")
    return small + swapped(small, "head")


def elementwise(gate_proj, up_proj, feats, keep_cols):
    rows, ff = gate_proj.shape
    tiles = keep_cols.shape[1]
    keep = jnp.broadcast_to(keep_cols.astype(F32)[:, :, None], (rows, tiles, TILE)).reshape(rows, ff)
    lifted = jnp.maximum(gate_proj, 0.0)
    squared = lifted * lifted
    act = squared * up_proj
    differ = act - feats.astype(F32)
    grad_act = keep * differ
    grad_gate = (grad_act * up_proj * 2.0 * lifted).astype(BF16)
    grad_up = (grad_act * squared).astype(BF16)
    inner = 3.0 * jnp.sum(grad_act * act, axis=1)
    return act.astype(BF16), grad_gate, grad_up, inner, jnp.sum(grad_act * differ)


def products(hidden, grad_gate, grad_up, weights):
    w_gate, w_up, w_down = weights
    contract = (((1,), (1,)), ((), ()))
    down = jnp.dot(hidden, w_down, preferred_element_type=F32)
    grad = lax.dot_general(grad_gate, w_gate, contract, preferred_element_type=F32)
    return down, grad + lax.dot_general(grad_up, w_up, contract, preferred_element_type=F32)


TURNS = ((0, 1, 2, 3), (1, 2, 3, 0), (2, 1, 0, 3), (3, 2, 1, 0))


def on_square(residual, norm_gain, weights, teacher_feats, keep_tiles):
    w_gate, w_up, _ = weights
    rows, d_ctx = residual.shape
    ff = w_gate.shape[1]
    z = lax.axis_index("ctx")
    hp = lax.axis_index(HP)
    pair = lax.axis_index("pair")
    low = z < 2

    tile = transposed(residual)
    own_wide = residual.astype(F32)
    mean = summed_over_hp(jnp.sum(own_wide * own_wide, axis=1)) / D
    tile, mean = lax.optimization_barrier((tile, mean))
    rms = jnp.sqrt(mean + 1e-05)[:, None]
    across = swapped(tile, "head")
    both = swapped(jnp.stack([tile, across]), "pair")
    gain = lax.dynamic_slice_in_dim(norm_gain, z * d_ctx, d_ctx, 0)
    resid = jnp.stack([tile, both[0], across, both[1]]).astype(F32)
    scaled = (resid * gain).astype(BF16).reshape(4 * rows, d_ctx)
    parts = [
        jnp.dot(scaled, w, preferred_element_type=F32).astype(BF16).reshape(4, rows, ff)
        for w in (w_gate, w_up)
    ]

    came = [[None, None], [None, None]]
    for s in range(3):
        for i in range(2):
            right = picked(parts[i], jnp.clip(3 - s + z, 0, 3) ^ hp)
            left = picked(parts[i], jnp.clip(s - 3 + z, 0, 3) ^ hp)
            if s > 0:
                right = (right.astype(F32) + came[i][0].astype(F32)).astype(BF16)
                left = (left.astype(F32) + came[i][1].astype(F32)).astype(BF16)
            right, left = lax.optimization_barrier((right, left))
            came[i] = [shifted(right, 1), shifted(left, -1)]
    gate_proj, up_proj = [
        (picked(parts[i], z ^ hp).astype(F32) + came[i][0].astype(F32) + came[i][1].astype(F32)) / rms
        for i in range(2)
    ]
    hidden, grad_gate, grad_up, inner, loss = elementwise(gate_proj, up_proj, teacher_feats, keep_tiles)
    owned = jnp.concatenate([hidden, grad_gate, grad_up], axis=1)

    right, left = [shifted(owned, 1)], [shifted(owned, -1)]
    for s in range(2):
        right.append(shifted(right[s], 1))
        left.append(shifted(left[s], -1))
    turns = [owned, jnp.where(low, left[0], right[0])]
    _, arrived = lax.optimization_barrier((turns[1], (left[1], right[1])))
    turns.append(jnp.where(low, *arrived))
    _, arrived = lax.optimization_barrier((turns[2], (left[2], right[2])))
    outer = jnp.where(low, *arrived)
    inward = jnp.where(low, right[0], left[0])
    turns.append(jnp.where((z == 0) | (z == 3), outer, inward))

    def brought_home(k, down, grad):
        keeps_down = pair == (k & 1)
        sent = jnp.where(keeps_down, grad, down).astype(BF16)
        half = jnp.where(keeps_down, down, grad) + swapped(sent, "pair").astype(F32)
        route = [(k ^ 2, k), (k ^ 1, k ^ 3)]
        whole = (half + lax.ppermute(half.astype(BF16), HP, route).astype(F32)).astype(BF16)
        return [
            lax.ppermute(whole, ("ctx",) + HP, [(4 * c + h, 4 * TURNS[c][k] + c) for c in range(4)])
            for h in (k, k ^ 3)
        ]

    home = []
    for k in range(4):
        block = turns[k]
        down, grad = products(block[:, :ff], block[:, ff : 2 * ff], block[:, 2 * ff :], weights)
        home.append(brought_home(k, down, grad))

    count = jnp.sum(keep_tiles.astype(F32)) * TILE
    small = jnp.concatenate([inner, loss[None], count[None], jnp.zeros(126, F32)])
    small = summed_over_hp(small)
    totals, _ = lax.optimization_barrier((small[rows:], turns[3]))
    for d in (1, 2):
        totals = totals + lax.ppermute(totals, "ctx", [(c, c ^ d) for c in range(4)])
    loss_value = (totals[0] / totals[1]).reshape(1)

    down, grad = [sum(h[i].astype(F32) for h in home) for i in range(2)]
    gain_own = lax.dynamic_slice_in_dim(norm_gain, hp * d_ctx, d_ctx, 0)
    layer_out = (own_wide + down).astype(BF16)
    inner_own = small[:rows][:, None] * rms
    slope = gain_own * grad / rms - own_wide * inner_own / (D * rms * rms * rms)
    return layer_out, loss_value, slope


def on_any(residual, norm_gain, weights, teacher_feats, keep_tiles):
    w_gate, w_up, _ = weights
    rows = residual.shape[0]
    d_ctx, ff = w_gate.shape
    tiles = keep_tiles.shape[1]
    n_ctx = lax.axis_size("ctx")
    z = lax.axis_index("ctx")
    hp = lax.axis_index(HP)
    keep_cols = jnp.pad(keep_tiles.astype(BF16), ((0, 0), (0, -tiles % 128)))
    marked = lax.all_gather(jnp.concatenate([teacher_feats, keep_cols], axis=1), "ctx", tiled=True)
    wide = lax.all_gather(residual, HP, axis=1, tiled=True)
    resid = lax.all_to_all(wide, "ctx", split_axis=1, concat_axis=0, tiled=True).astype(F32)
    gain = lax.dynamic_slice_in_dim(norm_gain, z * d_ctx, d_ctx, 0)
    rms = jnp.sqrt(lax.psum(jnp.sum(resid * resid, axis=1), "ctx") / D + 1e-05)
    scaled = (resid * gain).astype(BF16)
    inv = (1.0 / rms)[:, None]
    sums = [
        lax.psum(jnp.dot(scaled, w, preferred_element_type=F32).astype(BF16), "ctx").astype(F32) * inv
        for w in (w_gate, w_up)
    ]
    keep_cols = marked[:, ff : ff + tiles]
    *values, inner, loss = elementwise(sums[0], sums[1], marked[:, :ff], keep_cols)
    down, grad = products(*values, weights)
    count = jnp.sum(keep_cols.astype(F32)) * TILE
    small = lax.psum(jnp.concatenate([inner, loss[None], count[None]]), HP)
    loss_value = (small[-2] / small[-1]).reshape(1)

    def home(whole):
        routed = lax.all_to_all(whole.astype(BF16), "ctx", 0, 1, tiled=True)
        return lax.psum_scatter(routed, HP, scatter_dimension=1, tiled=True).astype(F32)

    own = residual.astype(F32)
    layer_out = (own + home(down)).astype(BF16)
    rms_own = lax.dynamic_slice_in_dim(rms, z * rows, rows, 0)[:, None]
    inner_own = rms_own * lax.dynamic_slice_in_dim(small, z * rows, rows, 0)[:, None]
    gain_own = lax.dynamic_slice_in_dim(norm_gain, hp * own.shape[1], own.shape[1], 0)
    slope = gain_own * home(grad) / rms_own - own * inner_own / (D * rms_own * rms_own * rms_own)
    return layer_out, loss_value, slope


def local(
    student_query,
    teacher_keys,
    teacher_values,
    band_span,
    residual_in,
    norm_gain,
    w_gate,
    w_up,
    w_down,
    teacher_feats,
    keep_tiles,
):
    attended = attention(student_query, teacher_keys, teacher_values, band_span)
    residual = (residual_in.astype(F32) + attended).astype(BF16)
    sizes = tuple(lax.axis_size(a) for a in ("ctx", "head", "pair"))
    finish = on_square if sizes == (4, 2, 2) else on_any
    return finish(residual, norm_gain, (w_gate, w_up, w_down), teacher_feats, keep_tiles)


def solution(mesh):
    rows = P(("groups", "ctx"), HP)
    in_specs = (
        rows, rows, rows, P(("groups", "ctx")), rows, P(),
        P("ctx", HP), P("ctx", HP), P(HP, "ctx"), rows, rows,
    )
    out_specs = (rows, P("groups"), rows)
    return jax.shard_map(local, mesh=mesh, in_specs=in_specs, out_specs=out_specs, check_vma=False)
```

```python
import math

import jax
import jax.numpy as jnp
from jax import lax
from jax.experimental.layout import Layout, with_layout_constraint
from jax.sharding import PartitionSpec as P

D = 4096
HEADS = 32
KV_HEADS = 8
HEAD_DIM = 128
TILE = 128
WINDOW = 1024
HP = ("head", "pair")
F32 = jnp.float32
BF16 = jnp.bfloat16


def passed_along(block, axis, distance):
    devices = range(lax.axis_size(axis))
    route = [(i - distance, i) for i in devices if i - distance in devices]
    return lax.ppermute(block, axis, route)


def swapped(block, axis):
    return lax.ppermute(block, axis, [(0, 1), (1, 0)])


def transposed(block):
    n = lax.axis_size("ctx")
    route = [(c * n + h, h * n + c) for c in range(n) for h in range(n)]
    return lax.ppermute(block, ("ctx",) + HP, route)


def attend_heads(query_part, key_rows, value_rows, allowed):
    scores = jnp.einsum("thd,sd->hts", query_part, key_rows, preferred_element_type=F32) * (
        1.0 / math.sqrt(HEAD_DIM)
    )
    masked = jnp.where(allowed[None], scores, -jnp.inf)
    highest = jnp.max(masked, axis=-1, keepdims=True)
    weights = jnp.exp(masked - highest)
    normalized = (weights / jnp.sum(weights, axis=-1, keepdims=True)).astype(BF16)
    return jnp.einsum("hts,sd->thd", normalized, value_rows, preferred_element_type=F32)


def attention(student_query, teacher_keys, teacher_values, band_span):
    rows = student_query.shape[0]
    kv_local = teacher_keys.shape[1] // HEAD_DIM
    group_size = HEADS // KV_HEADS
    ctx_index = lax.axis_index("ctx")
    paired = jnp.stack([teacher_keys, teacher_values])
    back = min(-(-WINDOW // rows), lax.axis_size("ctx") - 1)
    blocks = [paired] + [passed_along(paired, "ctx", d) for d in range(1, back + 1)]
    round_ids = jnp.arange(back + 1, dtype=jnp.int32)
    key_pos = (
        (ctx_index - round_ids)[:, None] * rows + jnp.arange(rows, dtype=jnp.int32)[None, :]
    ).reshape(-1)
    query_pos = ctx_index * rows + jnp.arange(rows, dtype=jnp.int32)
    distance = query_pos[:, None] - key_pos[None, :]
    allowed = (distance >= 0) & (distance < band_span[:, None]) & (key_pos[None, :] >= 0)
    all_blocks = jnp.concatenate(blocks, axis=1)
    outputs = []
    for kv_head in range(kv_local):
        cols = slice(kv_head * HEAD_DIM, (kv_head + 1) * HEAD_DIM)
        first = kv_head * group_size * HEAD_DIM
        query_part = student_query[:, first : first + group_size * HEAD_DIM]
        outputs.append(
            attend_heads(
                query_part.reshape(rows, group_size, HEAD_DIM),
                all_blocks[0][:, cols],
                all_blocks[1][:, cols],
                allowed,
            ).reshape(rows, group_size * HEAD_DIM)
        )
    return jnp.concatenate(outputs, axis=1)


def row_major(block):
    return with_layout_constraint(block, Layout(major_to_minor=tuple(range(block.ndim))))


def shifted(block, distance):
    return row_major(passed_along(row_major(block), "ctx", distance))


def picked(blocks, index):
    return lax.dynamic_index_in_dim(blocks, index, 0, keepdims=False)


def summed_over_hp(small):
    small = small + swapped(small, "pair")
    return small + swapped(small, "head")


def elementwise(gate_proj, up_proj, feats, keep_cols):
    rows, ff = gate_proj.shape
    tiles = keep_cols.shape[1]
    keep = jnp.broadcast_to(keep_cols.astype(F32)[:, :, None], (rows, tiles, TILE)).reshape(rows, ff)
    lifted = jnp.maximum(gate_proj, 0.0)
    squared = lifted * lifted
    act = squared * up_proj
    differ = act - feats.astype(F32)
    grad_act = keep * differ
    grad_gate = (grad_act * up_proj * 2.0 * lifted).astype(BF16)
    grad_up = (grad_act * squared).astype(BF16)
    inner = 3.0 * jnp.sum(grad_act * act, axis=1)
    return act.astype(BF16), grad_gate, grad_up, inner, jnp.sum(grad_act * differ)


def products(hidden, grad_gate, grad_up, weights):
    w_gate, w_up, w_down = weights
    contract = (((1,), (1,)), ((), ()))
    down = jnp.dot(hidden, w_down, preferred_element_type=F32)
    grad = lax.dot_general(grad_gate, w_gate, contract, preferred_element_type=F32)
    return down, grad + lax.dot_general(grad_up, w_up, contract, preferred_element_type=F32)


TURNS = ((0, 1, 2, 3), (1, 2, 3, 0), (2, 1, 0, 3), (3, 2, 1, 0))


def on_square(residual, norm_gain, weights, teacher_feats, keep_tiles):
    w_gate, w_up, _ = weights
    rows, d_ctx = residual.shape
    ff = w_gate.shape[1]
    z = lax.axis_index("ctx")
    hp = lax.axis_index(HP)
    pair = lax.axis_index("pair")
    low = z < 2

    tile = transposed(residual)
    own_wide = residual.astype(F32)
    mean = summed_over_hp(jnp.sum(own_wide * own_wide, axis=1)) / D
    tile, mean = lax.optimization_barrier((tile, mean))
    rms = jnp.sqrt(mean + 1e-05)[:, None]
    across = swapped(tile, "head")
    both = swapped(jnp.stack([tile, across]), "pair")
    gain = lax.dynamic_slice_in_dim(norm_gain, z * d_ctx, d_ctx, 0)
    resid = jnp.stack([tile, both[0], across, both[1]]).astype(F32)
    scaled = (resid * gain).astype(BF16).reshape(4 * rows, d_ctx)
    parts = [
        jnp.dot(scaled, w, preferred_element_type=F32).astype(BF16).reshape(4, rows, ff)
        for w in (w_gate, w_up)
    ]

    came = [[None, None], [None, None]]
    for s in range(3):
        for i in range(2):
            right = picked(parts[i], jnp.clip(3 - s + z, 0, 3) ^ hp)
            left = picked(parts[i], jnp.clip(s - 3 + z, 0, 3) ^ hp)
            if s > 0:
                right = (right.astype(F32) + came[i][0].astype(F32)).astype(BF16)
                left = (left.astype(F32) + came[i][1].astype(F32)).astype(BF16)
            right, left = lax.optimization_barrier((right, left))
            came[i] = [shifted(right, 1), shifted(left, -1)]
    gate_proj, up_proj = [
        (picked(parts[i], z ^ hp).astype(F32) + came[i][0].astype(F32) + came[i][1].astype(F32)) / rms
        for i in range(2)
    ]
    hidden, grad_gate, grad_up, inner, loss = elementwise(gate_proj, up_proj, teacher_feats, keep_tiles)
    owned = jnp.concatenate([hidden, grad_gate, grad_up], axis=1)

    right, left = [shifted(owned, 1)], [shifted(owned, -1)]
    for s in range(2):
        right.append(shifted(right[s], 1))
        left.append(shifted(left[s], -1))
    def brought_home(k, down, grad):
        keeps_down = pair == (k & 1)
        sent = jnp.where(keeps_down, grad, down).astype(BF16)
        half = jnp.where(keeps_down, down, grad) + swapped(sent, "pair").astype(F32)
        route = [(k ^ 2, k), (k ^ 1, k ^ 3)]
        whole = (half + lax.ppermute(half.astype(BF16), HP, route).astype(F32)).astype(BF16)
        return [
            lax.ppermute(whole, ("ctx",) + HP, [(4 * c + h, 4 * TURNS[c][k] + c) for c in range(4)])
            for h in (k, k ^ 3)
        ]

    def turn(k, block):
        down, grad = products(block[:, :ff], block[:, ff : 2 * ff], block[:, 2 * ff :], weights)
        return brought_home(k, down, grad)

    count = jnp.sum(keep_tiles.astype(F32)) * TILE
    small = jnp.concatenate([inner, loss[None], count[None], jnp.zeros(126, F32)])
    small = summed_over_hp(small)

    def over_ctx(part, d, after):
        met = lax.ppermute(part, "ctx", [(c, c ^ d) for c in range(4)])
        return part + lax.optimization_barrier((met, after))[0]

    home = [turn(0, owned)]
    small, arrived = lax.optimization_barrier((small, (left[0], right[0])))
    totals = small[rows:]
    block = jnp.where(low, *arrived)
    home.append(turn(1, block))
    totals = over_ctx(totals, 1, block)
    home, totals, arrived = lax.optimization_barrier((home, totals, (left[1], right[1])))
    block = jnp.where(low, *arrived)
    home.append(turn(2, block))
    totals = over_ctx(totals, 2, block)
    home[2], totals, arrived = lax.optimization_barrier((home[2], totals, (left[2], right[2])))
    outer = jnp.where(low, *arrived)
    inward = jnp.where(low, right[0], left[0])
    home.append(turn(3, jnp.where((z == 0) | (z == 3), outer, inward)))
    loss_value = (totals[0] / totals[1]).reshape(1)

    down, grad = [sum(h[i].astype(F32) for h in home) for i in range(2)]
    gain_own = lax.dynamic_slice_in_dim(norm_gain, hp * d_ctx, d_ctx, 0)
    layer_out = (own_wide + down).astype(BF16)
    inner_own = small[:rows][:, None] * rms
    slope = gain_own * grad / rms - own_wide * inner_own / (D * rms * rms * rms)
    return layer_out, loss_value, slope


def on_any(residual, norm_gain, weights, teacher_feats, keep_tiles):
    w_gate, w_up, _ = weights
    rows = residual.shape[0]
    d_ctx, ff = w_gate.shape
    tiles = keep_tiles.shape[1]
    n_ctx = lax.axis_size("ctx")
    z = lax.axis_index("ctx")
    hp = lax.axis_index(HP)
    keep_cols = jnp.pad(keep_tiles.astype(BF16), ((0, 0), (0, -tiles % 128)))
    marked = lax.all_gather(jnp.concatenate([teacher_feats, keep_cols], axis=1), "ctx", tiled=True)
    wide = lax.all_gather(residual, HP, axis=1, tiled=True)
    resid = lax.all_to_all(wide, "ctx", split_axis=1, concat_axis=0, tiled=True).astype(F32)
    gain = lax.dynamic_slice_in_dim(norm_gain, z * d_ctx, d_ctx, 0)
    rms = jnp.sqrt(lax.psum(jnp.sum(resid * resid, axis=1), "ctx") / D + 1e-05)
    scaled = (resid * gain).astype(BF16)
    inv = (1.0 / rms)[:, None]
    sums = [
        lax.psum(jnp.dot(scaled, w, preferred_element_type=F32).astype(BF16), "ctx").astype(F32) * inv
        for w in (w_gate, w_up)
    ]
    keep_cols = marked[:, ff : ff + tiles]
    *values, inner, loss = elementwise(sums[0], sums[1], marked[:, :ff], keep_cols)
    down, grad = products(*values, weights)
    count = jnp.sum(keep_cols.astype(F32)) * TILE
    small = lax.psum(jnp.concatenate([inner, loss[None], count[None]]), HP)
    loss_value = (small[-2] / small[-1]).reshape(1)

    def home(whole):
        routed = lax.all_to_all(whole.astype(BF16), "ctx", 0, 1, tiled=True)
        return lax.psum_scatter(routed, HP, scatter_dimension=1, tiled=True).astype(F32)

    own = residual.astype(F32)
    layer_out = (own + home(down)).astype(BF16)
    rms_own = lax.dynamic_slice_in_dim(rms, z * rows, rows, 0)[:, None]
    inner_own = rms_own * lax.dynamic_slice_in_dim(small, z * rows, rows, 0)[:, None]
    gain_own = lax.dynamic_slice_in_dim(norm_gain, hp * own.shape[1], own.shape[1], 0)
    slope = gain_own * home(grad) / rms_own - own * inner_own / (D * rms_own * rms_own * rms_own)
    return layer_out, loss_value, slope


def local(
    student_query,
    teacher_keys,
    teacher_values,
    band_span,
    residual_in,
    norm_gain,
    w_gate,
    w_up,
    w_down,
    teacher_feats,
    keep_tiles,
):
    attended = attention(student_query, teacher_keys, teacher_values, band_span)
    residual = (residual_in.astype(F32) + attended).astype(BF16)
    sizes = tuple(lax.axis_size(a) for a in ("ctx", "head", "pair"))
    finish = on_square if sizes == (4, 2, 2) else on_any
    return finish(residual, norm_gain, (w_gate, w_up, w_down), teacher_feats, keep_tiles)


def solution(mesh):
    rows = P(("groups", "ctx"), HP)
    in_specs = (
        rows, rows, rows, P(("groups", "ctx")), rows, P(),
        P("ctx", HP), P("ctx", HP), P(HP, "ctx"), rows, rows,
    )
    out_specs = (rows, P("groups"), rows)
    return jax.shard_map(local, mesh=mesh, in_specs=in_specs, out_specs=out_specs, check_vma=False)
```

```python
import math

import jax
import jax.numpy as jnp
from jax import lax
from jax.experimental.layout import Layout, with_layout_constraint
from jax.sharding import PartitionSpec as P


D = 4096
HEADS = 32
KV_HEADS = 8
HEAD_DIM = 128
TILE = 128
WINDOW = 1024
HP = ("head", "pair")
F32 = jnp.float32
BF16 = jnp.bfloat16


def passed_along(block, axis, distance):
    devices = range(lax.axis_size(axis))
    route = [(i - distance, i) for i in devices if i - distance in devices]
    return lax.ppermute(block, axis, route)


def swapped(block, axis):
    return lax.ppermute(block, axis, [(0, 1), (1, 0)])


def transposed(block):
    n = lax.axis_size("ctx")
    route = [(c * n + h, h * n + c) for c in range(n) for h in range(n)]
    return lax.ppermute(block, ("ctx",) + HP, route)


def attend_heads(query_part, key_rows, value_rows, allowed):
    scores = jnp.einsum("thd,sd->hts", query_part, key_rows, preferred_element_type=F32) * (
        1.0 / math.sqrt(HEAD_DIM)
    )
    masked = jnp.where(allowed[None], scores, -jnp.inf)
    highest = jnp.max(masked, axis=-1, keepdims=True)
    weights = jnp.exp(masked - highest)
    normalized = (weights / jnp.sum(weights, axis=-1, keepdims=True)).astype(BF16)
    return jnp.einsum("hts,sd->thd", normalized, value_rows, preferred_element_type=F32)


def attention(student_query, teacher_keys, teacher_values, band_span):
    rows = student_query.shape[0]
    kv_local = teacher_keys.shape[1] // HEAD_DIM
    group_size = HEADS // KV_HEADS
    ctx_index = lax.axis_index("ctx")
    paired = jnp.stack([teacher_keys, teacher_values])
    back = min(-(-WINDOW // rows), lax.axis_size("ctx") - 1)
    blocks = [paired] + [passed_along(paired, "ctx", d) for d in range(1, back + 1)]
    round_ids = jnp.arange(back + 1, dtype=jnp.int32)
    key_pos = (
        (ctx_index - round_ids)[:, None] * rows + jnp.arange(rows, dtype=jnp.int32)[None, :]
    ).reshape(-1)
    query_pos = ctx_index * rows + jnp.arange(rows, dtype=jnp.int32)
    distance = query_pos[:, None] - key_pos[None, :]
    allowed = (distance >= 0) & (distance < band_span[:, None]) & (key_pos[None, :] >= 0)
    all_blocks = jnp.concatenate(blocks, axis=1)
    outputs = []
    for kv_head in range(kv_local):
        cols = slice(kv_head * HEAD_DIM, (kv_head + 1) * HEAD_DIM)
        first = kv_head * group_size * HEAD_DIM
        query_part = student_query[:, first : first + group_size * HEAD_DIM]
        outputs.append(
            attend_heads(
                query_part.reshape(rows, group_size, HEAD_DIM),
                all_blocks[0][:, cols],
                all_blocks[1][:, cols],
                allowed,
            ).reshape(rows, group_size * HEAD_DIM)
        )
    return jnp.concatenate(outputs, axis=1)


def row_major(block):
    return with_layout_constraint(block, Layout(major_to_minor=tuple(range(block.ndim))))


def shifted(block, distance):
    return row_major(passed_along(row_major(block), "ctx", distance))


def picked(blocks, index):
    return lax.dynamic_index_in_dim(blocks, index, 0, keepdims=False)


def summed_over_hp(small):
    small = small + swapped(small, "pair")
    return small + swapped(small, "head")


def elementwise(gate_proj, up_proj, feats, keep_cols):
    rows, ff = gate_proj.shape
    tiles = keep_cols.shape[1]
    keep = jnp.broadcast_to(keep_cols.astype(F32)[:, :, None], (rows, tiles, TILE)).reshape(rows, ff)
    lifted = jnp.maximum(gate_proj, 0.0)
    squared = lifted * lifted
    act = squared * up_proj
    differ = act - feats.astype(F32)
    grad_act = keep * differ
    grad_gate = (grad_act * up_proj * 2.0 * lifted).astype(BF16)
    grad_up = (grad_act * squared).astype(BF16)
    inner = 3.0 * jnp.sum(grad_act * act, axis=1)
    return act.astype(BF16), grad_gate, grad_up, inner, jnp.sum(grad_act * differ)


def products(hidden, grad_gate, grad_up, weights):
    w_gate, w_up, w_down = weights
    contract = (((1,), (1,)), ((), ()))
    down = jnp.dot(hidden, w_down, preferred_element_type=F32)
    grad = lax.dot_general(grad_gate, w_gate, contract, preferred_element_type=F32)
    return down, grad + lax.dot_general(grad_up, w_up, contract, preferred_element_type=F32)


TURNS = ((0, 1, 2, 3), (1, 2, 3, 0), (2, 1, 0, 3), (3, 2, 1, 0))


def on_square(residual, norm_gain, weights, teacher_feats, keep_tiles):
    w_gate, w_up, _ = weights
    rows, d_ctx = residual.shape
    ff = w_gate.shape[1]
    z = lax.axis_index("ctx")
    hp = lax.axis_index(HP)
    pair = lax.axis_index("pair")
    low = z < 2

    tile = transposed(residual)
    own_wide = residual.astype(F32)
    mean = summed_over_hp(jnp.sum(own_wide * own_wide, axis=1)) / D
    tile, mean = lax.optimization_barrier((tile, mean))
    rms = jnp.sqrt(mean + 1e-05)[:, None]
    across = swapped(tile, "head")
    both = swapped(jnp.stack([tile, across]), "pair")
    gain = lax.dynamic_slice_in_dim(norm_gain, z * d_ctx, d_ctx, 0)
    resid = jnp.stack([tile, both[0], across, both[1]]).astype(F32)
    scaled = (resid * gain).astype(BF16).reshape(4 * rows, d_ctx)
    parts = [
        jnp.dot(scaled, w, preferred_element_type=F32).astype(BF16).reshape(4, rows, ff)
        for w in (w_gate, w_up)
    ]

    came = [[None, None], [None, None]]
    for s in range(3):
        for i in range(2):
            right = picked(parts[i], jnp.clip(3 - s + z, 0, 3) ^ hp)
            left = picked(parts[i], jnp.clip(s - 3 + z, 0, 3) ^ hp)
            if s > 0:
                right = (right.astype(F32) + came[i][0].astype(F32)).astype(BF16)
                left = (left.astype(F32) + came[i][1].astype(F32)).astype(BF16)
            right, left = lax.optimization_barrier((right, left))
            came[i] = [shifted(right, 1), shifted(left, -1)]
    gate_proj, up_proj = [
        (picked(parts[i], z ^ hp).astype(F32) + came[i][0].astype(F32) + came[i][1].astype(F32)) / rms
        for i in range(2)
    ]
    hidden, grad_gate, grad_up, inner, loss = elementwise(gate_proj, up_proj, teacher_feats, keep_tiles)

    streams = [hidden, jnp.concatenate([grad_gate, grad_up], axis=1)]
    right, left = [streams], [streams]
    for s in range(3):
        right.append([shifted(v, 1) for v in right[s]])
        left.append([shifted(v, -1) for v in left[s]])
    right, left = right[1:], left[1:]

    def reduced(k, down, grad):
        keeps_down = pair == (k & 1)
        sent = jnp.where(keeps_down, grad, down).astype(BF16)
        half = jnp.where(keeps_down, down, grad) + swapped(sent, "pair").astype(F32)
        route = [(k ^ 2, k), (k ^ 1, k ^ 3)]
        return sent, (half + lax.ppermute(half.astype(BF16), HP, route).astype(F32)).astype(BF16)

    def brought_home(k, whole):
        return [
            lax.ppermute(whole, ("ctx",) + HP, [(4 * c + h, 4 * TURNS[c][k] + c) for c in range(4)])
            for h in (k, k ^ 3)
        ]

    def turn(k, values):
        both = values[1]
        return reduced(k, *products(values[0], both[:, :ff], both[:, ff:], weights))

    def chosen(a, b):
        return [jnp.where(low, v, w) for v, w in zip(a, b)]

    count = jnp.sum(keep_tiles.astype(F32)) * TILE
    small = jnp.concatenate([inner, loss[None], count[None], jnp.zeros(126, F32)])
    small = summed_over_hp(small)

    home, values = [], streams
    ends = (z == 0) | (z == 3)
    for k in range(4):
        if k == 1:
            values = chosen(left[0], right[0])
        if k > 1:
            _, arrived = lax.optimization_barrier((values, (left[k - 1], right[k - 1])))
            values = chosen(*arrived)
        if k == 3:
            inward = chosen(right[0], left[0])
            values = [jnp.where(ends, v, w) for v, w in zip(values, inward)]
        sent, whole = turn(k, values)
        home.append(brought_home(k, whole))
    part, _ = lax.optimization_barrier((small[rows:], sent))
    totals = part + sum(lax.ppermute(part, "ctx", [(c, c ^ d) for c in range(4)]) for d in (1, 2, 3))
    loss_value = (totals[0] / totals[1]).reshape(1)

    down, grad = [sum(h[i].astype(F32) for h in home) for i in range(2)]
    gain_own = lax.dynamic_slice_in_dim(norm_gain, hp * d_ctx, d_ctx, 0)
    layer_out = (own_wide + down).astype(BF16)
    inner_own = small[:rows][:, None] * rms
    slope = gain_own * grad / rms - own_wide * inner_own / (D * rms * rms * rms)
    return layer_out, loss_value, slope


def on_any(residual, norm_gain, weights, teacher_feats, keep_tiles):
    w_gate, w_up, _ = weights
    rows = residual.shape[0]
    d_ctx, ff = w_gate.shape
    tiles = keep_tiles.shape[1]
    z = lax.axis_index("ctx")
    hp = lax.axis_index(HP)
    keep_cols = jnp.pad(keep_tiles.astype(BF16), ((0, 0), (0, -tiles % 128)))
    marked = lax.all_gather(jnp.concatenate([teacher_feats, keep_cols], axis=1), "ctx", tiled=True)
    wide = lax.all_gather(residual, HP, axis=1, tiled=True)
    resid = lax.all_to_all(wide, "ctx", split_axis=1, concat_axis=0, tiled=True).astype(F32)
    gain = lax.dynamic_slice_in_dim(norm_gain, z * d_ctx, d_ctx, 0)
    rms = jnp.sqrt(lax.psum(jnp.sum(resid * resid, axis=1), "ctx") / D + 1e-05)
    scaled = (resid * gain).astype(BF16)
    inv = (1.0 / rms)[:, None]
    sums = [
        lax.psum(jnp.dot(scaled, w, preferred_element_type=F32).astype(BF16), "ctx").astype(F32) * inv
        for w in (w_gate, w_up)
    ]
    keep_cols = marked[:, ff : ff + tiles]
    *values, inner, loss = elementwise(sums[0], sums[1], marked[:, :ff], keep_cols)
    down, grad = products(*values, weights)
    count = jnp.sum(keep_cols.astype(F32)) * TILE
    small = lax.psum(jnp.concatenate([inner, loss[None], count[None]]), HP)
    loss_value = (small[-2] / small[-1]).reshape(1)

    def home(whole):
        routed = lax.all_to_all(whole.astype(BF16), "ctx", 0, 1, tiled=True)
        return lax.psum_scatter(routed, HP, scatter_dimension=1, tiled=True).astype(F32)

    own = residual.astype(F32)
    layer_out = (own + home(down)).astype(BF16)
    rms_own = lax.dynamic_slice_in_dim(rms, z * rows, rows, 0)[:, None]
    inner_own = rms_own * lax.dynamic_slice_in_dim(small, z * rows, rows, 0)[:, None]
    gain_own = lax.dynamic_slice_in_dim(norm_gain, hp * own.shape[1], own.shape[1], 0)
    slope = gain_own * home(grad) / rms_own - own * inner_own / (D * rms_own * rms_own * rms_own)
    return layer_out, loss_value, slope


def local(
    student_query,
    teacher_keys,
    teacher_values,
    band_span,
    residual_in,
    norm_gain,
    w_gate,
    w_up,
    w_down,
    teacher_feats,
    keep_tiles,
):
    attended = attention(student_query, teacher_keys, teacher_values, band_span)
    residual = (residual_in.astype(F32) + attended).astype(BF16)
    sizes = tuple(lax.axis_size(a) for a in ("ctx", "head", "pair"))
    weights = (w_gate, w_up, w_down)
    if sizes == (4, 2, 2):
        return on_square(residual, norm_gain, weights, teacher_feats, keep_tiles)
    return on_any(residual, norm_gain, weights, teacher_feats, keep_tiles)


def solution(mesh):
    rows = P(("groups", "ctx"), HP)
    in_specs = (
        rows, rows, rows, P(("groups", "ctx")), rows, P(),
        P("ctx", HP), P("ctx", HP), P(HP, "ctx"), rows, rows,
    )
    out_specs = (rows, P("groups"), rows)
    return jax.shard_map(local, mesh=mesh, in_specs=in_specs, out_specs=out_specs, check_vma=False)
```

```python
import math

import jax
import jax.numpy as jnp
from jax import lax
from jax.experimental.layout import Layout, with_layout_constraint
from jax.sharding import PartitionSpec as P


D = 4096
HEADS = 32
KV_HEADS = 8
HEAD_DIM = 128
TILE = 128
WINDOW = 1024
HP = ("head", "pair")
F32 = jnp.float32
BF16 = jnp.bfloat16


def passed_along(block, axis, distance):
    devices = range(lax.axis_size(axis))
    route = [(i - distance, i) for i in devices if i - distance in devices]
    return lax.ppermute(block, axis, route)


def swapped(block, axis):
    return lax.ppermute(block, axis, [(0, 1), (1, 0)])


def transposed(block):
    n = lax.axis_size("ctx")
    route = [(c * n + h, h * n + c) for c in range(n) for h in range(n)]
    return lax.ppermute(block, ("ctx",) + HP, route)


def attend_heads(query_part, key_rows, value_rows, allowed):
    scores = jnp.einsum("thd,sd->hts", query_part, key_rows, preferred_element_type=F32) * (
        1.0 / math.sqrt(HEAD_DIM)
    )
    masked = jnp.where(allowed[None], scores, -jnp.inf)
    highest = jnp.max(masked, axis=-1, keepdims=True)
    weights = jnp.exp(masked - highest)
    normalized = (weights / jnp.sum(weights, axis=-1, keepdims=True)).astype(BF16)
    return jnp.einsum("hts,sd->thd", normalized, value_rows, preferred_element_type=F32)


def attention(student_query, teacher_keys, teacher_values, band_span):
    rows = student_query.shape[0]
    kv_local = teacher_keys.shape[1] // HEAD_DIM
    group_size = HEADS // KV_HEADS
    ctx_index = lax.axis_index("ctx")
    paired = jnp.stack([teacher_keys, teacher_values])
    back = min(-(-WINDOW // rows), lax.axis_size("ctx") - 1)
    blocks = [paired] + [passed_along(paired, "ctx", d) for d in range(1, back + 1)]
    round_ids = jnp.arange(back + 1, dtype=jnp.int32)
    key_pos = (
        (ctx_index - round_ids)[:, None] * rows + jnp.arange(rows, dtype=jnp.int32)[None, :]
    ).reshape(-1)
    query_pos = ctx_index * rows + jnp.arange(rows, dtype=jnp.int32)
    distance = query_pos[:, None] - key_pos[None, :]
    allowed = (distance >= 0) & (distance < band_span[:, None]) & (key_pos[None, :] >= 0)
    all_blocks = jnp.concatenate(blocks, axis=1)
    outputs = []
    for kv_head in range(kv_local):
        cols = slice(kv_head * HEAD_DIM, (kv_head + 1) * HEAD_DIM)
        first = kv_head * group_size * HEAD_DIM
        query_part = student_query[:, first : first + group_size * HEAD_DIM]
        outputs.append(
            attend_heads(
                query_part.reshape(rows, group_size, HEAD_DIM),
                all_blocks[0][:, cols],
                all_blocks[1][:, cols],
                allowed,
            ).reshape(rows, group_size * HEAD_DIM)
        )
    return jnp.concatenate(outputs, axis=1)


def row_major(block):
    return with_layout_constraint(block, Layout(major_to_minor=tuple(range(block.ndim))))


def shifted(block, distance):
    return row_major(passed_along(row_major(block), "ctx", distance))


def picked(blocks, index):
    return lax.dynamic_index_in_dim(blocks, index, 0, keepdims=False)


def summed_over_hp(small):
    small = small + swapped(small, "pair")
    return small + swapped(small, "head")


def elementwise(gate_proj, up_proj, feats, keep_cols, first_hidden=False):
    rows, ff = gate_proj.shape
    tiles = keep_cols.shape[1]
    keep = jnp.broadcast_to(keep_cols.astype(F32)[:, :, None], (rows, tiles, TILE)).reshape(rows, ff)
    lifted = jnp.maximum(gate_proj, 0.0)
    squared = lifted * lifted
    act = squared * up_proj
    hidden = act.astype(BF16)
    if first_hidden:
        hidden, lifted, squared, up_proj, act = lax.optimization_barrier(
            (hidden, lifted, squared, up_proj, act)
        )
    differ = act - feats.astype(F32)
    grad_act = keep * differ
    grad_gate = (grad_act * up_proj * 2.0 * lifted).astype(BF16)
    grad_up = (grad_act * squared).astype(BF16)
    inner = 3.0 * jnp.sum(grad_act * act, axis=1)
    return hidden, grad_gate, grad_up, inner, jnp.sum(grad_act * differ)


def products(hidden, grad_gate, grad_up, weights):
    w_gate, w_up, w_down = weights
    contract = (((1,), (1,)), ((), ()))
    down = jnp.dot(hidden, w_down, preferred_element_type=F32)
    grad = lax.dot_general(grad_gate, w_gate, contract, preferred_element_type=F32)
    return down, grad + lax.dot_general(grad_up, w_up, contract, preferred_element_type=F32)


TURNS = ((0, 1, 2, 3), (1, 2, 3, 0), (2, 1, 0, 3), (3, 2, 1, 0))


def on_square(residual, norm_gain, weights, teacher_feats, keep_tiles):
    w_gate, w_up, _ = weights
    rows, d_ctx = residual.shape
    ff = w_gate.shape[1]
    z = lax.axis_index("ctx")
    hp = lax.axis_index(HP)
    pair = lax.axis_index("pair")
    low = z < 2

    tile = transposed(residual)
    own_wide = residual.astype(F32)
    mean = summed_over_hp(jnp.sum(own_wide * own_wide, axis=1)) / D
    tile, mean = lax.optimization_barrier((tile, mean))
    rms = jnp.sqrt(mean + 1e-05)[:, None]
    across = swapped(tile, "head")
    both = swapped(jnp.stack([tile, across]), "pair")
    gain = lax.dynamic_slice_in_dim(norm_gain, z * d_ctx, d_ctx, 0)
    resid = jnp.stack([tile, both[0], across, both[1]]).astype(F32)
    scaled = (resid * gain).astype(BF16).reshape(4 * rows, d_ctx)

    def projected(w):
        return jnp.dot(scaled, w, preferred_element_type=F32).astype(BF16).reshape(4, rows, ff)

    parts = [projected(w_gate)]
    came = [None, None]
    for s in range(3):
        for i in range(2):
            if s == 0 and i == 1:
                scaled, _ = lax.optimization_barrier((scaled, right))
                parts.append(projected(w_up))
            if s > 0:
                came[i], _ = lax.optimization_barrier((came[i], right))
            right = picked(parts[i], jnp.clip(3 - s + z, 0, 3) ^ hp)
            left = picked(parts[i], jnp.clip(s - 3 + z, 0, 3) ^ hp)
            if s > 0:
                right = (right.astype(F32) + came[i][0].astype(F32)).astype(BF16)
                left = (left.astype(F32) + came[i][1].astype(F32)).astype(BF16)
            right, left = lax.optimization_barrier((right, left))
            came[i] = [shifted(right, 1), shifted(left, -1)]
    gate_proj, up_proj = [
        (picked(parts[i], z ^ hp).astype(F32) + came[i][0].astype(F32) + came[i][1].astype(F32)) / rms
        for i in range(2)
    ]
    hidden, grad_gate, grad_up, inner, loss = elementwise(
        gate_proj, up_proj, teacher_feats, keep_tiles, True
    )

    streams = [hidden, jnp.concatenate([grad_gate, grad_up], axis=1)]
    right, left = [streams], [streams]
    for s in range(3):
        right.append([shifted(v, 1) for v in right[s]])
        left.append([shifted(v, -1) for v in left[s]])
    right, left = right[1:], left[1:]

    def reduced(k, down, grad):
        keeps_down = pair == (k & 1)
        sent = jnp.where(keeps_down, grad, down).astype(BF16)
        half = jnp.where(keeps_down, down, grad) + swapped(sent, "pair").astype(F32)
        route = [(k ^ 2, k), (k ^ 1, k ^ 3)]
        return sent, (half + lax.ppermute(half.astype(BF16), HP, route).astype(F32)).astype(BF16)

    def brought_home(k, whole):
        return [
            lax.ppermute(whole, ("ctx",) + HP, [(4 * c + h, 4 * TURNS[c][k] + c) for c in range(4)])
            for h in (k, k ^ 3)
        ]

    def turn(k, values):
        both = values[1]
        return reduced(k, *products(values[0], both[:, :ff], both[:, ff:], weights))

    def chosen(a, b):
        return [jnp.where(low, v, w) for v, w in zip(a, b)]

    count = jnp.sum(keep_tiles.astype(F32)) * TILE
    small = jnp.concatenate([inner, loss[None], count[None], jnp.zeros(126, F32)])
    small = summed_over_hp(small)

    home, values = [], streams
    ends = (z == 0) | (z == 3)
    for k in range(4):
        if k == 1:
            values = chosen(left[0], right[0])
        if k > 1:
            _, arrived = lax.optimization_barrier((values, (left[k - 1], right[k - 1])))
            values = chosen(*arrived)
        if k == 3:
            inward = chosen(right[0], left[0])
            values = [jnp.where(ends, v, w) for v, w in zip(values, inward)]
        sent, whole = turn(k, values)
        home.append(brought_home(k, whole))
    part, _ = lax.optimization_barrier((small[rows:], sent))
    totals = part + sum(lax.ppermute(part, "ctx", [(c, c ^ d) for c in range(4)]) for d in (1, 2, 3))
    loss_value = (totals[0] / totals[1]).reshape(1)

    down, grad = [sum(h[i].astype(F32) for h in home) for i in range(2)]
    gain_own = lax.dynamic_slice_in_dim(norm_gain, hp * d_ctx, d_ctx, 0)
    layer_out = (own_wide + down).astype(BF16)
    inner_own = small[:rows][:, None] * rms
    slope = gain_own * grad / rms - own_wide * inner_own / (D * rms * rms * rms)
    return layer_out, loss_value, slope


def on_any(residual, norm_gain, weights, teacher_feats, keep_tiles):
    w_gate, w_up, _ = weights
    rows = residual.shape[0]
    d_ctx, ff = w_gate.shape
    tiles = keep_tiles.shape[1]
    z = lax.axis_index("ctx")
    hp = lax.axis_index(HP)
    keep_cols = jnp.pad(keep_tiles.astype(BF16), ((0, 0), (0, -tiles % 128)))
    marked = lax.all_gather(jnp.concatenate([teacher_feats, keep_cols], axis=1), "ctx", tiled=True)
    wide = lax.all_gather(residual, HP, axis=1, tiled=True)
    resid = lax.all_to_all(wide, "ctx", split_axis=1, concat_axis=0, tiled=True).astype(F32)
    gain = lax.dynamic_slice_in_dim(norm_gain, z * d_ctx, d_ctx, 0)
    rms = jnp.sqrt(lax.psum(jnp.sum(resid * resid, axis=1), "ctx") / D + 1e-05)
    scaled = (resid * gain).astype(BF16)
    inv = (1.0 / rms)[:, None]
    sums = [
        lax.psum(jnp.dot(scaled, w, preferred_element_type=F32).astype(BF16), "ctx").astype(F32) * inv
        for w in (w_gate, w_up)
    ]
    keep_cols = marked[:, ff : ff + tiles]
    *values, inner, loss = elementwise(sums[0], sums[1], marked[:, :ff], keep_cols)
    down, grad = products(*values, weights)
    count = jnp.sum(keep_cols.astype(F32)) * TILE
    small = lax.psum(jnp.concatenate([inner, loss[None], count[None]]), HP)
    loss_value = (small[-2] / small[-1]).reshape(1)

    def home(whole):
        routed = lax.all_to_all(whole.astype(BF16), "ctx", 0, 1, tiled=True)
        return lax.psum_scatter(routed, HP, scatter_dimension=1, tiled=True).astype(F32)

    own = residual.astype(F32)
    layer_out = (own + home(down)).astype(BF16)
    rms_own = lax.dynamic_slice_in_dim(rms, z * rows, rows, 0)[:, None]
    inner_own = rms_own * lax.dynamic_slice_in_dim(small, z * rows, rows, 0)[:, None]
    gain_own = lax.dynamic_slice_in_dim(norm_gain, hp * own.shape[1], own.shape[1], 0)
    slope = gain_own * home(grad) / rms_own - own * inner_own / (D * rms_own * rms_own * rms_own)
    return layer_out, loss_value, slope


def local(
    student_query,
    teacher_keys,
    teacher_values,
    band_span,
    residual_in,
    norm_gain,
    w_gate,
    w_up,
    w_down,
    teacher_feats,
    keep_tiles,
):
    attended = attention(student_query, teacher_keys, teacher_values, band_span)
    residual = (residual_in.astype(F32) + attended).astype(BF16)
    sizes = tuple(lax.axis_size(a) for a in ("ctx", "head", "pair"))
    weights = (w_gate, w_up, w_down)
    if sizes == (4, 2, 2):
        return on_square(residual, norm_gain, weights, teacher_feats, keep_tiles)
    return on_any(residual, norm_gain, weights, teacher_feats, keep_tiles)


def solution(mesh):
    rows = P(("groups", "ctx"), HP)
    in_specs = (
        rows, rows, rows, P(("groups", "ctx")), rows, P(),
        P("ctx", HP), P("ctx", HP), P(HP, "ctx"), rows, rows,
    )
    out_specs = (rows, P("groups"), rows)
    return jax.shard_map(local, mesh=mesh, in_specs=in_specs, out_specs=out_specs, check_vma=False)
```

```python
import math

import jax
import jax.numpy as jnp
from jax import lax
from jax.experimental import pallas as pl
from jax.experimental.layout import Layout, with_layout_constraint
from jax.experimental.pallas import tpu as pltpu
from jax.sharding import PartitionSpec as P


D = 4096
HEADS = 32
KV_HEADS = 8
HEAD_DIM = 128
TILE = 128
WINDOW = 1024
HP = ("head", "pair")
F32 = jnp.float32
BF16 = jnp.bfloat16


def passed_along(block, axis, distance):
    devices = range(lax.axis_size(axis))
    route = [(i - distance, i) for i in devices if i - distance in devices]
    return lax.ppermute(block, axis, route)


def swapped(block, axis):
    return lax.ppermute(block, axis, [(0, 1), (1, 0)])


def transposed(block):
    n = lax.axis_size("ctx")
    route = [(c * n + h, h * n + c) for c in range(n) for h in range(n)]
    return lax.ppermute(block, ("ctx",) + HP, route)


def attention_kernel(ctx_ref, query_ref, span_ref, resid_ref, *refs):
    *pair_refs, out_ref = refs
    rows = query_ref.shape[0]
    kv_local = pair_refs[0].shape[2] // HEAD_DIM
    group_size = HEADS // KV_HEADS
    ctx = ctx_ref[0]
    shape = (rows, rows)
    offset = lax.broadcasted_iota(jnp.int32, shape, 0) - lax.broadcasted_iota(jnp.int32, shape, 1)
    span = span_ref[...]
    allowed = []
    for back in range(len(pair_refs)):
        distance = offset + back * rows
        reach = jnp.where(ctx >= back, span, 0)
        allowed.append((distance >= 0) & (distance < reach))
    allowed = jnp.concatenate([jnp.where(v, 0.0, -jnp.inf) for v in allowed], axis=1)
    for kv_head in range(kv_local):
        cols = slice(kv_head * HEAD_DIM, (kv_head + 1) * HEAD_DIM)
        keys = jnp.concatenate([r[0, :, cols] for r in pair_refs], axis=0)
        values = jnp.concatenate([r[1, :, cols] for r in pair_refs], axis=0)
        for g in range(group_size):
            first = (kv_head * group_size + g) * HEAD_DIM
            head = slice(first, first + HEAD_DIM)
            scores = lax.dot_general(
                query_ref[:, head], keys, (((1,), (1,)), ((), ())), preferred_element_type=F32
            )
            masked = scores * (1.0 / math.sqrt(HEAD_DIM)) + allowed
            weights = jnp.exp(masked - jnp.max(masked, axis=1, keepdims=True))
            normalized = weights * (1.0 / jnp.sum(weights, axis=1, keepdims=True))
            mixed = jnp.dot(normalized.astype(BF16), values, preferred_element_type=F32)
            out_ref[:, head] = (resid_ref[:, head].astype(F32) + mixed).astype(BF16)


def attended_residual(student_query, teacher_keys, teacher_values, band_span, residual_in):
    rows = student_query.shape[0]
    paired = jnp.stack([teacher_keys, teacher_values])
    back = min(-(-WINDOW // rows), lax.axis_size("ctx") - 1)
    blocks = [paired] + [passed_along(paired, "ctx", d) for d in range(1, back + 1)]
    whole = pl.BlockSpec(memory_space=pltpu.VMEM)
    return pl.pallas_call(
        attention_kernel,
        out_shape=jax.ShapeDtypeStruct(residual_in.shape, BF16),
        in_specs=[pl.BlockSpec(memory_space=pltpu.SMEM)] + [whole] * (3 + len(blocks)),
        out_specs=whole,
        name="attention",
    )(lax.axis_index("ctx")[None], student_query, band_span[:, None], residual_in, *blocks)


def row_major(block):
    return with_layout_constraint(block, Layout(major_to_minor=tuple(range(block.ndim))))


def shifted(block, distance):
    return row_major(passed_along(row_major(block), "ctx", distance))


def picked(blocks, index):
    return lax.dynamic_index_in_dim(blocks, index, 0, keepdims=False)


def summed_over_hp(small):
    small = small + swapped(small, "pair")
    return small + swapped(small, "head")


def elementwise(gate_proj, up_proj, feats, keep_cols, first_hidden=False):
    rows, ff = gate_proj.shape
    tiles = keep_cols.shape[1]
    keep = jnp.broadcast_to(keep_cols.astype(F32)[:, :, None], (rows, tiles, TILE)).reshape(rows, ff)
    lifted = jnp.maximum(gate_proj, 0.0)
    squared = lifted * lifted
    act = squared * up_proj
    hidden = act.astype(BF16)
    if first_hidden:
        hidden, lifted, squared, up_proj, act = lax.optimization_barrier(
            (hidden, lifted, squared, up_proj, act)
        )
    differ = act - feats.astype(F32)
    grad_act = keep * differ
    grad_gate = (grad_act * up_proj * 2.0 * lifted).astype(BF16)
    grad_up = (grad_act * squared).astype(BF16)
    inner = 3.0 * jnp.sum(grad_act * act, axis=1)
    return hidden, grad_gate, grad_up, inner, jnp.sum(grad_act * differ)


def products(hidden, grad_gate, grad_up, weights):
    w_gate, w_up, w_down = weights
    contract = (((1,), (1,)), ((), ()))
    down = jnp.dot(hidden, w_down, preferred_element_type=F32)
    grad = lax.dot_general(grad_gate, w_gate, contract, preferred_element_type=F32)
    return down, grad + lax.dot_general(grad_up, w_up, contract, preferred_element_type=F32)


TURNS = ((0, 1, 2, 3), (1, 2, 3, 0), (2, 1, 0, 3), (3, 2, 1, 0))


def on_square(residual, norm_gain, weights, teacher_feats, keep_tiles):
    w_gate, w_up, _ = weights
    rows, d_ctx = residual.shape
    ff = w_gate.shape[1]
    z = lax.axis_index("ctx")
    hp = lax.axis_index(HP)
    pair = lax.axis_index("pair")
    low = z < 2

    tile = transposed(residual)
    own_wide = residual.astype(F32)
    mean = summed_over_hp(jnp.sum(own_wide * own_wide, axis=1)) / D
    tile, mean = lax.optimization_barrier((tile, mean))
    rms = jnp.sqrt(mean + 1e-05)[:, None]
    across = swapped(tile, "head")
    both = swapped(jnp.stack([tile, across]), "pair")
    gain = lax.dynamic_slice_in_dim(norm_gain, z * d_ctx, d_ctx, 0)
    resid = jnp.stack([tile, both[0], across, both[1]]).astype(F32)
    scaled = (resid * gain).astype(BF16)
    scaled = scaled.reshape(4, rows, d_ctx)

    def projected(blocks, w):
        return jnp.dot(blocks, w, preferred_element_type=F32).astype(BF16)

    farthest = picked(scaled, jnp.where(low, 3, 0) ^ hp)
    came = [None, None]
    for s in range(3):
        for i, w in enumerate((w_gate, w_up)):
            if s == 0:
                if i == 1:
                    farthest, scaled, _ = lax.optimization_barrier((farthest, scaled, right))
                right = left = projected(farthest, w)
            else:
                if (s, i) == (1, 0):
                    scaled, _ = lax.optimization_barrier((scaled, right))
                    blocks = scaled.reshape(4 * rows, d_ctx)
                    parts = [projected(blocks, v).reshape(4, rows, ff) for v in (w_gate, w_up)]
                    came[0], parts[1] = lax.optimization_barrier((came[0], parts[1]))
                came[i], _ = lax.optimization_barrier((came[i], right))
                right = picked(parts[i], jnp.clip(3 - s + z, 0, 3) ^ hp)
                left = picked(parts[i], jnp.clip(s - 3 + z, 0, 3) ^ hp)
                right = (right.astype(F32) + came[i][0].astype(F32)).astype(BF16)
                left = (left.astype(F32) + came[i][1].astype(F32)).astype(BF16)
            right, left = lax.optimization_barrier((right, left))
            came[i] = [shifted(right, 1), shifted(left, -1)]
    gate_proj, up_proj = [
        (picked(parts[i], z ^ hp).astype(F32) + came[i][0].astype(F32) + came[i][1].astype(F32)) / rms
        for i in range(2)
    ]
    hidden, grad_gate, grad_up, inner, loss = elementwise(
        gate_proj, up_proj, teacher_feats, keep_tiles, True
    )

    streams = [hidden, jnp.concatenate([grad_gate, grad_up], axis=1)]
    right, left = [streams], [streams]
    for s in range(3):
        right.append([shifted(v, 1) for v in right[s]])
        left.append([shifted(v, -1) for v in left[s]])
    right, left = right[1:], left[1:]

    def reduced(k, down, grad):
        keeps_down = pair == (k & 1)
        sent = jnp.where(keeps_down, grad, down).astype(BF16)
        half = jnp.where(keeps_down, down, grad) + swapped(sent, "pair").astype(F32)
        route = [(k ^ 2, k), (k ^ 1, k ^ 3)]
        return sent, (half + lax.ppermute(half.astype(BF16), HP, route).astype(F32)).astype(BF16)

    def brought_home(k, whole):
        return [
            lax.ppermute(whole, ("ctx",) + HP, [(4 * c + h, 4 * TURNS[c][k] + c) for c in range(4)])
            for h in (k, k ^ 3)
        ]

    def turn(k, values):
        both = values[1]
        return reduced(k, *products(values[0], both[:, :ff], both[:, ff:], weights))

    def chosen(a, b):
        return [jnp.where(low, v, w) for v, w in zip(a, b)]

    count = jnp.sum(keep_tiles.astype(F32)) * TILE
    small = jnp.concatenate([inner, loss[None], count[None], jnp.zeros(126, F32)])
    small = summed_over_hp(small)

    home, values = [], streams
    ends = (z == 0) | (z == 3)
    for k in range(4):
        if k == 1:
            values = chosen(left[0], right[0])
        if k > 1:
            _, arrived = lax.optimization_barrier((values, (left[k - 1], right[k - 1])))
            values = chosen(*arrived)
        if k == 3:
            inward = chosen(right[0], left[0])
            values = [jnp.where(ends, v, w) for v, w in zip(values, inward)]
        sent, whole = turn(k, values)
        home.append(brought_home(k, whole))
    part, _ = lax.optimization_barrier((small[rows:], sent))
    totals = part + sum(lax.ppermute(part, "ctx", [(c, c ^ d) for c in range(4)]) for d in (1, 2, 3))
    loss_value = (totals[0] / totals[1]).reshape(1)

    down, grad = [sum(h[i].astype(F32) for h in home) for i in range(2)]
    gain_own = lax.dynamic_slice_in_dim(norm_gain, hp * d_ctx, d_ctx, 0)
    layer_out = (own_wide + down).astype(BF16)
    inner_own = small[:rows][:, None] * rms
    slope = gain_own * grad / rms - own_wide * inner_own / (D * rms * rms * rms)
    return layer_out, loss_value, slope


def on_any(residual, norm_gain, weights, teacher_feats, keep_tiles):
    w_gate, w_up, _ = weights
    rows = residual.shape[0]
    d_ctx, ff = w_gate.shape
    tiles = keep_tiles.shape[1]
    z = lax.axis_index("ctx")
    hp = lax.axis_index(HP)
    keep_cols = jnp.pad(keep_tiles.astype(BF16), ((0, 0), (0, -tiles % 128)))
    marked = lax.all_gather(jnp.concatenate([teacher_feats, keep_cols], axis=1), "ctx", tiled=True)
    wide = lax.all_gather(residual, HP, axis=1, tiled=True)
    resid = lax.all_to_all(wide, "ctx", split_axis=1, concat_axis=0, tiled=True).astype(F32)
    gain = lax.dynamic_slice_in_dim(norm_gain, z * d_ctx, d_ctx, 0)
    rms = jnp.sqrt(lax.psum(jnp.sum(resid * resid, axis=1), "ctx") / D + 1e-05)
    scaled = (resid * gain).astype(BF16)
    inv = (1.0 / rms)[:, None]
    sums = [
        lax.psum(jnp.dot(scaled, w, preferred_element_type=F32).astype(BF16), "ctx").astype(F32) * inv
        for w in (w_gate, w_up)
    ]
    keep_cols = marked[:, ff : ff + tiles]
    *values, inner, loss = elementwise(sums[0], sums[1], marked[:, :ff], keep_cols)
    down, grad = products(*values, weights)
    count = jnp.sum(keep_cols.astype(F32)) * TILE
    small = lax.psum(jnp.concatenate([inner, loss[None], count[None]]), HP)
    loss_value = (small[-2] / small[-1]).reshape(1)

    def home(whole):
        routed = lax.all_to_all(whole.astype(BF16), "ctx", 0, 1, tiled=True)
        return lax.psum_scatter(routed, HP, scatter_dimension=1, tiled=True).astype(F32)

    own = residual.astype(F32)
    layer_out = (own + home(down)).astype(BF16)
    rms_own = lax.dynamic_slice_in_dim(rms, z * rows, rows, 0)[:, None]
    inner_own = rms_own * lax.dynamic_slice_in_dim(small, z * rows, rows, 0)[:, None]
    gain_own = lax.dynamic_slice_in_dim(norm_gain, hp * own.shape[1], own.shape[1], 0)
    slope = gain_own * home(grad) / rms_own - own * inner_own / (D * rms_own * rms_own * rms_own)
    return layer_out, loss_value, slope


def local(
    student_query,
    teacher_keys,
    teacher_values,
    band_span,
    residual_in,
    norm_gain,
    w_gate,
    w_up,
    w_down,
    teacher_feats,
    keep_tiles,
):
    residual = attended_residual(student_query, teacher_keys, teacher_values, band_span, residual_in)
    sizes = tuple(lax.axis_size(a) for a in ("ctx", "head", "pair"))
    weights = (w_gate, w_up, w_down)
    if sizes == (4, 2, 2):
        return on_square(residual, norm_gain, weights, teacher_feats, keep_tiles)
    return on_any(residual, norm_gain, weights, teacher_feats, keep_tiles)


def solution(mesh):
    rows = P(("groups", "ctx"), HP)
    in_specs = (
        rows, rows, rows, P(("groups", "ctx")), rows, P(),
        P("ctx", HP), P("ctx", HP), P(HP, "ctx"), rows, rows,
    )
    out_specs = (rows, P("groups"), rows)
    return jax.shard_map(local, mesh=mesh, in_specs=in_specs, out_specs=out_specs, check_vma=False)
```

```python
import math

import jax
import jax.numpy as jnp
from jax import lax
from jax.experimental.layout import Layout, with_layout_constraint
from jax.sharding import PartitionSpec as P


D = 4096
HEADS = 32
KV_HEADS = 8
HEAD_DIM = 128
TILE = 128
WINDOW = 1024
HP = ("head", "pair")
F32 = jnp.float32
BF16 = jnp.bfloat16


def passed_along(block, axis, distance):
    devices = range(lax.axis_size(axis))
    route = [(i - distance, i) for i in devices if i - distance in devices]
    return lax.ppermute(block, axis, route)


def swapped(block, axis):
    return lax.ppermute(block, axis, [(0, 1), (1, 0)])


def transposed(block):
    n = lax.axis_size("ctx")
    route = [(c * n + h, h * n + c) for c in range(n) for h in range(n)]
    return lax.ppermute(block, ("ctx",) + HP, route)


def attend_heads(query_part, key_rows, value_rows, allowed):
    scores = jnp.einsum("thd,sd->hts", query_part, key_rows, preferred_element_type=F32) * (
        1.0 / math.sqrt(HEAD_DIM)
    )
    masked = jnp.where(allowed[None], scores, -jnp.inf)
    highest = jnp.max(masked, axis=-1, keepdims=True)
    weights = jnp.exp(masked - highest)
    normalized = (weights / jnp.sum(weights, axis=-1, keepdims=True)).astype(BF16)
    return jnp.einsum("hts,sd->thd", normalized, value_rows, preferred_element_type=F32)


def attention(student_query, teacher_keys, teacher_values, band_span):
    rows = student_query.shape[0]
    kv_local = teacher_keys.shape[1] // HEAD_DIM
    group_size = HEADS // KV_HEADS
    ctx_index = lax.axis_index("ctx")
    paired = jnp.stack([teacher_keys, teacher_values])
    back = min(-(-WINDOW // rows), lax.axis_size("ctx") - 1)
    blocks = [paired] + [passed_along(paired, "ctx", d) for d in range(1, back + 1)]
    round_ids = jnp.arange(back + 1, dtype=jnp.int32)
    key_pos = (
        (ctx_index - round_ids)[:, None] * rows + jnp.arange(rows, dtype=jnp.int32)[None, :]
    ).reshape(-1)
    query_pos = ctx_index * rows + jnp.arange(rows, dtype=jnp.int32)
    distance = query_pos[:, None] - key_pos[None, :]
    allowed = (distance >= 0) & (distance < band_span[:, None]) & (key_pos[None, :] >= 0)
    all_blocks = jnp.concatenate(blocks, axis=1)
    outputs = []
    for kv_head in range(kv_local):
        cols = slice(kv_head * HEAD_DIM, (kv_head + 1) * HEAD_DIM)
        first = kv_head * group_size * HEAD_DIM
        query_part = student_query[:, first : first + group_size * HEAD_DIM]
        outputs.append(
            attend_heads(
                query_part.reshape(rows, group_size, HEAD_DIM),
                all_blocks[0][:, cols],
                all_blocks[1][:, cols],
                allowed,
            ).reshape(rows, group_size * HEAD_DIM)
        )
    return jnp.concatenate(outputs, axis=1)


def row_major(block):
    return with_layout_constraint(block, Layout(major_to_minor=tuple(range(block.ndim))))


def shifted(block, distance):
    return row_major(passed_along(row_major(block), "ctx", distance))


def picked(blocks, index):
    return lax.dynamic_index_in_dim(blocks, index, 0, keepdims=False)


def summed_over_hp(small):
    small = small + swapped(small, "pair")
    return small + swapped(small, "head")


def elementwise(gate_proj, up_proj, feats, keep_cols, first_hidden=False):
    rows, ff = gate_proj.shape
    tiles = keep_cols.shape[1]
    keep = jnp.broadcast_to(keep_cols.astype(F32)[:, :, None], (rows, tiles, TILE)).reshape(rows, ff)
    lifted = jnp.maximum(gate_proj, 0.0)
    squared = lifted * lifted
    act = squared * up_proj
    hidden = act.astype(BF16)
    if first_hidden:
        hidden, lifted, squared, up_proj, act = lax.optimization_barrier(
            (hidden, lifted, squared, up_proj, act)
        )
    differ = act - feats.astype(F32)
    grad_act = keep * differ
    grad_gate = (grad_act * up_proj * 2.0 * lifted).astype(BF16)
    grad_up = (grad_act * squared).astype(BF16)
    inner = 3.0 * jnp.sum(grad_act * act, axis=1)
    loss = jnp.sum(grad_act * differ)
    return hidden, grad_gate, grad_up, inner, loss


def down_product(hidden, weights):
    return jnp.dot(hidden, weights[2], preferred_element_type=F32)


def grad_product(grad_gate, grad_up, weights):
    contract = (((1,), (1,)), ((), ()))
    grad = lax.dot_general(grad_gate, weights[0], contract, preferred_element_type=F32)
    return grad + lax.dot_general(grad_up, weights[1], contract, preferred_element_type=F32)


TURNS = ((0, 1, 2, 3), (1, 2, 3, 0), (2, 1, 0, 3), (3, 2, 1, 0))


def on_square(residual, norm_gain, weights, teacher_feats, keep_tiles):
    w_gate, w_up, _ = weights
    rows, d_ctx = residual.shape
    ff = w_gate.shape[1]
    z = lax.axis_index("ctx")
    hp = lax.axis_index(HP)
    pair = lax.axis_index("pair")
    low = z < 2

    tile = transposed(residual)
    own_wide = residual.astype(F32)
    mean = summed_over_hp(jnp.sum(own_wide * own_wide, axis=1)) / D
    tile, mean = lax.optimization_barrier((tile, mean))
    rms = jnp.sqrt(mean + 1e-05)[:, None]
    across = swapped(tile, "head")
    both = swapped(jnp.stack([tile, across]), "pair")
    gain = lax.dynamic_slice_in_dim(norm_gain, z * d_ctx, d_ctx, 0)
    resid = jnp.stack([tile, both[0], across, both[1]]).astype(F32)
    scaled = (resid * gain).astype(BF16).reshape(4 * rows, d_ctx)

    def projected(w):
        return jnp.dot(scaled, w, preferred_element_type=F32).astype(BF16).reshape(4, rows, ff)

    parts = [projected(w_gate)]
    came = [None, None]
    for s in range(3):
        for i in range(2):
            if s == 0 and i == 1:
                scaled, _ = lax.optimization_barrier((scaled, right))
                parts.append(projected(w_up))
            if s > 0:
                came[i], _ = lax.optimization_barrier((came[i], (left, right)))
            right = picked(parts[i], jnp.clip(3 - s + z, 0, 3) ^ hp)
            left = picked(parts[i], jnp.clip(s - 3 + z, 0, 3) ^ hp)
            if s > 0:
                right = (right.astype(F32) + came[i][0].astype(F32)).astype(BF16)
                left = (left.astype(F32) + came[i][1].astype(F32)).astype(BF16)
            right, left = lax.optimization_barrier((right, left))
            came[i] = [shifted(right, 1), shifted(left, -1)]
    gate_proj, up_proj = [
        (picked(parts[i], z ^ hp).astype(F32) + came[i][0].astype(F32) + came[i][1].astype(F32)) / rms
        for i in range(2)
    ]
    hidden, grad_gate, grad_up, inner, loss = elementwise(
        gate_proj, up_proj, teacher_feats, keep_tiles, True
    )

    streams = [hidden, jnp.concatenate([grad_gate, grad_up], axis=1)]
    right, left = [streams], [streams]
    for s in range(3):
        sent = [shifted(right[s][0], 1)], [shifted(left[s][0], -1)]
        right.append(sent[0] + [shifted(right[s][1], 1)])
        left.append(sent[1] + [shifted(left[s][1], -1)])
    right, left = right[1:], left[1:]

    def reduced(k, down, grad):
        keeps_down = pair == (k & 1)
        sent = jnp.where(keeps_down, grad, down).astype(BF16)
        half = jnp.where(keeps_down, down, grad) + swapped(sent, "pair").astype(F32)
        route = [(k ^ 2, k), (k ^ 1, k ^ 3)]
        return sent, (half + lax.ppermute(half.astype(BF16), HP, route).astype(F32)).astype(BF16)

    def brought_home(k, whole):
        return [
            lax.ppermute(whole, ("ctx",) + HP, [(4 * c + h, 4 * TURNS[c][k] + c) for c in range(4)])
            for h in (k, k ^ 3)
        ]

    count = jnp.sum(keep_tiles.astype(F32)) * TILE
    small = jnp.concatenate([inner, loss[None], count[None], jnp.zeros(126, F32)])
    small = summed_over_hp(small)

    ends = (z == 0) | (z == 3)

    def chosen(k, i, before):
        if k == 0:
            return streams[i]
        arrived = (left[k - 1][i], right[k - 1][i])
        if k > 1:
            _, arrived = lax.optimization_barrier((before, arrived))
        value = jnp.where(low, *arrived)
        if k == 3:
            value = jnp.where(ends, value, jnp.where(low, right[0][i], left[0][i]))
        return value

    home, values = [], [None, None]
    for k in range(4):
        values[0] = chosen(k, 0, values[0])
        down = down_product(values[0], weights)
        values[1] = chosen(k, 1, values[1])
        grad = grad_product(values[1][:, :ff], values[1][:, ff:], weights)
        sent, whole = reduced(k, down, grad)
        home.append(brought_home(k, whole))
    part, _ = lax.optimization_barrier((small[rows:], sent))
    totals = part + sum(lax.ppermute(part, "ctx", [(c, c ^ d) for c in range(4)]) for d in (1, 2, 3))
    loss_value = (totals[0] / totals[1]).reshape(1)

    down, grad = [sum(h[i].astype(F32) for h in home) for i in range(2)]
    gain_own = lax.dynamic_slice_in_dim(norm_gain, hp * d_ctx, d_ctx, 0)
    layer_out = (own_wide + down).astype(BF16)
    inner_own = small[:rows][:, None] * rms
    slope = gain_own * grad / rms - own_wide * inner_own / (D * rms * rms * rms)
    return layer_out, loss_value, slope


def on_any(residual, norm_gain, weights, teacher_feats, keep_tiles):
    w_gate, w_up, _ = weights
    rows = residual.shape[0]
    d_ctx, ff = w_gate.shape
    tiles = keep_tiles.shape[1]
    z = lax.axis_index("ctx")
    hp = lax.axis_index(HP)
    keep_cols = jnp.pad(keep_tiles.astype(BF16), ((0, 0), (0, -tiles % 128)))
    marked = lax.all_gather(jnp.concatenate([teacher_feats, keep_cols], axis=1), "ctx", tiled=True)
    wide = lax.all_gather(residual, HP, axis=1, tiled=True)
    resid = lax.all_to_all(wide, "ctx", split_axis=1, concat_axis=0, tiled=True).astype(F32)
    gain = lax.dynamic_slice_in_dim(norm_gain, z * d_ctx, d_ctx, 0)
    rms = jnp.sqrt(lax.psum(jnp.sum(resid * resid, axis=1), "ctx") / D + 1e-05)
    scaled = (resid * gain).astype(BF16)
    inv = (1.0 / rms)[:, None]
    sums = [
        lax.psum(jnp.dot(scaled, w, preferred_element_type=F32).astype(BF16), "ctx").astype(F32) * inv
        for w in (w_gate, w_up)
    ]
    keep_cols = marked[:, ff : ff + tiles]
    *values, inner, loss = elementwise(sums[0], sums[1], marked[:, :ff], keep_cols)
    down, grad = down_product(values[0], weights), grad_product(*values[1:], weights)
    count = jnp.sum(keep_cols.astype(F32)) * TILE
    small = lax.psum(jnp.concatenate([inner, loss[None], count[None]]), HP)
    loss_value = (small[-2] / small[-1]).reshape(1)

    def home(whole):
        routed = lax.all_to_all(whole.astype(BF16), "ctx", 0, 1, tiled=True)
        return lax.psum_scatter(routed, HP, scatter_dimension=1, tiled=True).astype(F32)

    own = residual.astype(F32)
    layer_out = (own + home(down)).astype(BF16)
    rms_own = lax.dynamic_slice_in_dim(rms, z * rows, rows, 0)[:, None]
    inner_own = rms_own * lax.dynamic_slice_in_dim(small, z * rows, rows, 0)[:, None]
    gain_own = lax.dynamic_slice_in_dim(norm_gain, hp * own.shape[1], own.shape[1], 0)
    slope = gain_own * home(grad) / rms_own - own * inner_own / (D * rms_own * rms_own * rms_own)
    return layer_out, loss_value, slope


def local(
    student_query,
    teacher_keys,
    teacher_values,
    band_span,
    residual_in,
    norm_gain,
    w_gate,
    w_up,
    w_down,
    teacher_feats,
    keep_tiles,
):
    attended = attention(student_query, teacher_keys, teacher_values, band_span)
    residual = (residual_in.astype(F32) + attended).astype(BF16)
    sizes = tuple(lax.axis_size(a) for a in ("ctx", "head", "pair"))
    weights = (w_gate, w_up, w_down)
    if sizes == (4, 2, 2):
        return on_square(residual, norm_gain, weights, teacher_feats, keep_tiles)
    return on_any(residual, norm_gain, weights, teacher_feats, keep_tiles)


def solution(mesh):
    rows = P(("groups", "ctx"), HP)
    in_specs = (
        rows, rows, rows, P(("groups", "ctx")), rows, P(),
        P("ctx", HP), P("ctx", HP), P(HP, "ctx"), rows, rows,
    )
    out_specs = (rows, P("groups"), rows)
    return jax.shard_map(local, mesh=mesh, in_specs=in_specs, out_specs=out_specs, check_vma=False)
```

```python
import math

import jax
import jax.numpy as jnp
from jax import lax
from jax.experimental.layout import Layout, with_layout_constraint
from jax.sharding import PartitionSpec as P


D = 4096
HEADS = 32
KV_HEADS = 8
HEAD_DIM = 128
TILE = 128
WINDOW = 1024
HP = ("head", "pair")
F32 = jnp.float32
BF16 = jnp.bfloat16


def passed_along(block, axis, distance):
    devices = range(lax.axis_size(axis))
    route = [(i - distance, i) for i in devices if i - distance in devices]
    return lax.ppermute(block, axis, route)


def swapped(block, axis):
    return lax.ppermute(block, axis, [(0, 1), (1, 0)])


def transposed(block):
    n = lax.axis_size("ctx")
    route = [(c * n + h, h * n + c) for c in range(n) for h in range(n)]
    return lax.ppermute(block, ("ctx",) + HP, route)


def attend_heads(query_part, key_rows, value_rows, allowed):
    scores = jnp.einsum("thd,sd->hts", query_part, key_rows, preferred_element_type=F32) * (
        1.0 / math.sqrt(HEAD_DIM)
    )
    masked = jnp.where(allowed[None], scores, -jnp.inf)
    highest = jnp.max(masked, axis=-1, keepdims=True)
    weights = jnp.exp(masked - highest)
    normalized = (weights / jnp.sum(weights, axis=-1, keepdims=True)).astype(BF16)
    return jnp.einsum("hts,sd->thd", normalized, value_rows, preferred_element_type=F32)


def attention(student_query, teacher_keys, teacher_values, band_span):
    rows = student_query.shape[0]
    kv_local = teacher_keys.shape[1] // HEAD_DIM
    group_size = HEADS // KV_HEADS
    ctx_index = lax.axis_index("ctx")
    paired = jnp.stack([teacher_keys, teacher_values])
    back = min(-(-WINDOW // rows), lax.axis_size("ctx") - 1)
    blocks = [paired] + [passed_along(paired, "ctx", d) for d in range(1, back + 1)]
    round_ids = jnp.arange(back + 1, dtype=jnp.int32)
    key_pos = (
        (ctx_index - round_ids)[:, None] * rows + jnp.arange(rows, dtype=jnp.int32)[None, :]
    ).reshape(-1)
    query_pos = ctx_index * rows + jnp.arange(rows, dtype=jnp.int32)
    distance = query_pos[:, None] - key_pos[None, :]
    allowed = (distance >= 0) & (distance < band_span[:, None]) & (key_pos[None, :] >= 0)
    all_blocks = jnp.concatenate(blocks, axis=1)
    outputs = []
    for kv_head in range(kv_local):
        cols = slice(kv_head * HEAD_DIM, (kv_head + 1) * HEAD_DIM)
        first = kv_head * group_size * HEAD_DIM
        query_part = student_query[:, first : first + group_size * HEAD_DIM]
        outputs.append(
            attend_heads(
                query_part.reshape(rows, group_size, HEAD_DIM),
                all_blocks[0][:, cols],
                all_blocks[1][:, cols],
                allowed,
            ).reshape(rows, group_size * HEAD_DIM)
        )
    return jnp.concatenate(outputs, axis=1)


def row_major(block):
    return with_layout_constraint(block, Layout(major_to_minor=tuple(range(block.ndim))))


def shifted(block, distance):
    return row_major(passed_along(row_major(block), "ctx", distance))


def picked(blocks, index):
    return lax.dynamic_index_in_dim(blocks, index, 0, keepdims=False)


def summed_over_hp(small):
    small = small + swapped(small, "pair")
    return small + swapped(small, "head")


def elementwise(gate_proj, up_proj, feats, keep_cols, first_hidden=False):
    rows, ff = gate_proj.shape
    tiles = keep_cols.shape[1]
    keep = jnp.broadcast_to(keep_cols.astype(F32)[:, :, None], (rows, tiles, TILE)).reshape(rows, ff)
    lifted = jnp.maximum(gate_proj, 0.0)
    squared = lifted * lifted
    act = squared * up_proj
    hidden = act.astype(BF16)
    if first_hidden:
        hidden, lifted, squared, up_proj, act = lax.optimization_barrier(
            (hidden, lifted, squared, up_proj, act)
        )
    differ = act - feats.astype(F32)
    grad_act = keep * differ
    grad_gate = (grad_act * up_proj * 2.0 * lifted).astype(BF16)
    grad_up = (grad_act * squared).astype(BF16)
    inner = 3.0 * jnp.sum(grad_act * act, axis=1)
    loss = jnp.sum(grad_act * differ)
    return hidden, grad_gate, grad_up, inner, loss


def down_product(hidden, weights):
    return jnp.dot(hidden, weights[2], preferred_element_type=F32)


def grad_product(grad_gate, grad_up, weights):
    contract = (((1,), (1,)), ((), ()))
    grad = lax.dot_general(grad_gate, weights[0], contract, preferred_element_type=F32)
    return grad + lax.dot_general(grad_up, weights[1], contract, preferred_element_type=F32)


TURNS = ((0, 1, 2, 3), (1, 2, 3, 0), (2, 1, 0, 3), (3, 2, 1, 0))


def on_square(residual, norm_gain, weights, teacher_feats, keep_tiles):
    w_gate, w_up, _ = weights
    rows, d_ctx = residual.shape
    ff = w_gate.shape[1]
    z = lax.axis_index("ctx")
    hp = lax.axis_index(HP)
    pair = lax.axis_index("pair")
    low = z < 2

    tile = transposed(residual)
    own_wide = residual.astype(F32)
    mean = summed_over_hp(jnp.sum(own_wide * own_wide, axis=1)) / D
    tile, mean = lax.optimization_barrier((tile, mean))
    rms = jnp.sqrt(mean + 1e-05)[:, None]
    across = swapped(tile, "head")
    both = swapped(jnp.stack([tile, across]), "pair")
    gain = lax.dynamic_slice_in_dim(norm_gain, z * d_ctx, d_ctx, 0)
    resid = jnp.stack([tile, both[0], across, both[1]]).astype(F32)
    scaled = (resid * gain).astype(BF16)
    scaled = scaled.reshape(4, rows, d_ctx)

    def projected(blocks, w):
        return jnp.dot(blocks, w, preferred_element_type=F32).astype(BF16)

    farthest = picked(scaled, jnp.where(low, 3, 0) ^ hp)
    came = [None, None]
    for s in range(3):
        for i, w in enumerate((w_gate, w_up)):
            if s == 0:
                if i == 1:
                    farthest, scaled, _ = lax.optimization_barrier((farthest, scaled, right))
                right = left = projected(farthest, w)
            else:
                if (s, i) == (1, 0):
                    scaled, _ = lax.optimization_barrier((scaled, right))
                    blocks = scaled.reshape(4 * rows, d_ctx)
                    parts = [projected(blocks, v).reshape(4, rows, ff) for v in (w_gate, w_up)]
                    came[0], parts[1] = lax.optimization_barrier((came[0], parts[1]))
                came[i], _ = lax.optimization_barrier((came[i], (left, right)))
                right = picked(parts[i], jnp.clip(3 - s + z, 0, 3) ^ hp)
                left = picked(parts[i], jnp.clip(s - 3 + z, 0, 3) ^ hp)
                right = (right.astype(F32) + came[i][0].astype(F32)).astype(BF16)
                left = (left.astype(F32) + came[i][1].astype(F32)).astype(BF16)
            right, left = lax.optimization_barrier((right, left))
            came[i] = [shifted(right, 1), shifted(left, -1)]
    gate_proj, up_proj = [
        (picked(parts[i], z ^ hp).astype(F32) + came[i][0].astype(F32) + came[i][1].astype(F32)) / rms
        for i in range(2)
    ]
    hidden, grad_gate, grad_up, inner, loss = elementwise(
        gate_proj, up_proj, teacher_feats, keep_tiles, True
    )

    streams = [hidden, jnp.concatenate([grad_gate, grad_up], axis=1)]
    right, left = [streams], [streams]
    for s in range(3):
        sent = [shifted(right[s][0], 1)], [shifted(left[s][0], -1)]
        right.append(sent[0] + [shifted(right[s][1], 1)])
        left.append(sent[1] + [shifted(left[s][1], -1)])
    right, left = right[1:], left[1:]

    def reduced(k, down, grad):
        keeps_down = pair == (k & 1)
        sent = jnp.where(keeps_down, grad, down).astype(BF16)
        half = jnp.where(keeps_down, down, grad) + swapped(sent, "pair").astype(F32)
        route = [(k ^ 2, k), (k ^ 1, k ^ 3)]
        return sent, (half + lax.ppermute(half.astype(BF16), HP, route).astype(F32)).astype(BF16)

    def brought_home(k, whole):
        return [
            lax.ppermute(whole, ("ctx",) + HP, [(4 * c + h, 4 * TURNS[c][k] + c) for c in range(4)])
            for h in (k, k ^ 3)
        ]

    count = jnp.sum(keep_tiles.astype(F32)) * TILE
    small = jnp.concatenate([inner, loss[None], count[None], jnp.zeros(126, F32)])
    small = summed_over_hp(small)

    ends = (z == 0) | (z == 3)

    def chosen(k, i, before):
        if k == 0:
            return streams[i]
        arrived = (left[k - 1][i], right[k - 1][i])
        if k > 1:
            _, arrived = lax.optimization_barrier((before, arrived))
        value = jnp.where(low, *arrived)
        if k == 3:
            value = jnp.where(ends, value, jnp.where(low, right[0][i], left[0][i]))
        return value

    home, values = [], [None, None]
    for k in range(4):
        values[0] = chosen(k, 0, values[0])
        down = down_product(values[0], weights)
        values[1] = chosen(k, 1, values[1])
        grad = grad_product(values[1][:, :ff], values[1][:, ff:], weights)
        sent, whole = reduced(k, down, grad)
        home.append(brought_home(k, whole))
    part, _ = lax.optimization_barrier((small[rows:], sent))
    totals = part + sum(lax.ppermute(part, "ctx", [(c, c ^ d) for c in range(4)]) for d in (1, 2, 3))
    loss_value = (totals[0] / totals[1]).reshape(1)

    down, grad = [sum(h[i].astype(F32) for h in home) for i in range(2)]
    gain_own = lax.dynamic_slice_in_dim(norm_gain, hp * d_ctx, d_ctx, 0)
    layer_out = (own_wide + down).astype(BF16)
    inner_own = small[:rows][:, None] * rms
    slope = gain_own * grad / rms - own_wide * inner_own / (D * rms * rms * rms)
    return layer_out, loss_value, slope


def on_any(residual, norm_gain, weights, teacher_feats, keep_tiles):
    w_gate, w_up, _ = weights
    rows = residual.shape[0]
    d_ctx, ff = w_gate.shape
    tiles = keep_tiles.shape[1]
    z = lax.axis_index("ctx")
    hp = lax.axis_index(HP)
    keep_cols = jnp.pad(keep_tiles.astype(BF16), ((0, 0), (0, -tiles % 128)))
    marked = lax.all_gather(jnp.concatenate([teacher_feats, keep_cols], axis=1), "ctx", tiled=True)
    wide = lax.all_gather(residual, HP, axis=1, tiled=True)
    resid = lax.all_to_all(wide, "ctx", split_axis=1, concat_axis=0, tiled=True).astype(F32)
    gain = lax.dynamic_slice_in_dim(norm_gain, z * d_ctx, d_ctx, 0)
    rms = jnp.sqrt(lax.psum(jnp.sum(resid * resid, axis=1), "ctx") / D + 1e-05)
    scaled = (resid * gain).astype(BF16)
    inv = (1.0 / rms)[:, None]
    sums = [
        lax.psum(jnp.dot(scaled, w, preferred_element_type=F32).astype(BF16), "ctx").astype(F32) * inv
        for w in (w_gate, w_up)
    ]
    keep_cols = marked[:, ff : ff + tiles]
    *values, inner, loss = elementwise(sums[0], sums[1], marked[:, :ff], keep_cols)
    down, grad = down_product(values[0], weights), grad_product(*values[1:], weights)
    count = jnp.sum(keep_cols.astype(F32)) * TILE
    small = lax.psum(jnp.concatenate([inner, loss[None], count[None]]), HP)
    loss_value = (small[-2] / small[-1]).reshape(1)

    def home(whole):
        routed = lax.all_to_all(whole.astype(BF16), "ctx", 0, 1, tiled=True)
        return lax.psum_scatter(routed, HP, scatter_dimension=1, tiled=True).astype(F32)

    own = residual.astype(F32)
    layer_out = (own + home(down)).astype(BF16)
    rms_own = lax.dynamic_slice_in_dim(rms, z * rows, rows, 0)[:, None]
    inner_own = rms_own * lax.dynamic_slice_in_dim(small, z * rows, rows, 0)[:, None]
    gain_own = lax.dynamic_slice_in_dim(norm_gain, hp * own.shape[1], own.shape[1], 0)
    slope = gain_own * home(grad) / rms_own - own * inner_own / (D * rms_own * rms_own * rms_own)
    return layer_out, loss_value, slope


def local(
    student_query,
    teacher_keys,
    teacher_values,
    band_span,
    residual_in,
    norm_gain,
    w_gate,
    w_up,
    w_down,
    teacher_feats,
    keep_tiles,
):
    attended = attention(student_query, teacher_keys, teacher_values, band_span)
    residual = (residual_in.astype(F32) + attended).astype(BF16)
    sizes = tuple(lax.axis_size(a) for a in ("ctx", "head", "pair"))
    weights = (w_gate, w_up, w_down)
    if sizes == (4, 2, 2):
        return on_square(residual, norm_gain, weights, teacher_feats, keep_tiles)
    return on_any(residual, norm_gain, weights, teacher_feats, keep_tiles)


def solution(mesh):
    rows = P(("groups", "ctx"), HP)
    in_specs = (
        rows, rows, rows, P(("groups", "ctx")), rows, P(),
        P("ctx", HP), P("ctx", HP), P(HP, "ctx"), rows, rows,
    )
    out_specs = (rows, P("groups"), rows)
    return jax.shard_map(local, mesh=mesh, in_specs=in_specs, out_specs=out_specs, check_vma=False)
```
